512 devices in a mesh: emit: 32 (over x, z), vx: 8 (over y), vy: 2 (over core).
Axes of the slice: x: 4, y: 8, z: 8, core: 2. Of those that a mesh axis runs over, the one named last changes fastest.
Arguments:
- fwd_state: float32 [3, 32, 2048, 512], P(None, 'emit', 'vx', 'vy'), may hold values from -6 to 6
- adj_state: float32 [3, 32, 2048, 512], P(None, 'emit', 'vx', 'vy'), may hold values from -6 to 6
- courant: float32 [2048, 512], P('vx', 'vy'), may hold values from 0.2 to 0.45
- decay_rate: float32 [2048, 512], P('vx', 'vy'), may hold values from 0.2 to 0.9
- strength: float32 [2048, 512], P('vx', 'vy'), may hold values from 0.05 to 0.4
- footprint: int32 [32, 8, 2, 16], P('emit', 'vx', 'vy'), may hold values from 0 to 31, all different within a row
- owner_map: int32 [8, 2, 32], P('vx', 'vy'), may hold values from 0 to 31, each once within a row
Outputs:
- gradient: float32 [32, 128, 256], P('emit', 'vx', 'vy')
- pressure: float32 [32, 2048, 512], P('emit', 'vx', 'vy')
The draws below stay inside these ranges and needn't reach their ends.
Inputs may be any that keep to these rules, and one draw needn't show every extreme that they name: `footprint`: in each row the 16 ids are distinct block ids of one tile. `owner_map`: for each tile a permutation of its 32 block ids.
All inputs are finite; a program needn't handle non-finite values.
Results may differ from the reference program's by a relative error of at most 0.0003.
Values sent between devices are 32-bit elements; how exact they have to be, the bound alone decides.
No kernel may reach another device: no remote copies, remote signals or barrier semaphores. Data moves between devices by JAX's collectives and lax.ppermute only.
A program may use at most 64 MiB of HBM per device.

```python
import jax
import jax.numpy as jnp
from jax import lax

BR = 16
BC = 128
BX = 16
BY = 2
STEPS = 4
NB = 32
FP = 16
GROUPS = 32
NX = 2048
NY = 512
N_VX = 8
N_VY = 2


def block_levels(own_key, extent, pieces, smallest, largest):
    gain = 1.0
    for axis_at, shards_of in pieces:
        steps = jax.random.uniform(jax.random.fold_in(jax.random.fold_in(own_key, 6), axis_at), (shards_of,), jnp.float32, smallest / len(pieces), largest / len(pieces))
        gain = gain * jnp.repeat(jnp.exp(steps), extent[axis_at] // shards_of).reshape((-1,) + (1,) * (len(extent) - 1 - axis_at))
    return gain


def different_ones(key, rows, amount, top, lift):
    order = jax.random.permutation(jax.random.fold_in(key, 1), amount)
    favour = order
    for power in range(3):
        favour = favour * favour // amount
    favour = favour * lift // amount
    chance = jax.random.randint(jax.random.fold_in(key, 2), (rows, amount), 0, 4096) + favour
    fixed_rows = jax.random.permutation(jax.random.fold_in(key, 3), rows)[jnp.arange(amount) % rows]
    chance = jnp.where(jnp.arange(rows)[:, None] == fixed_rows[None, :], 1 << 14, chance)
    score = chance * amount + jnp.arange(amount)
    return lax.top_k(score.astype(jnp.int32), top)[1].astype(jnp.int32)


def noise(rng, shape, width, reach, split=(), held_as=jnp.bfloat16):
    factor_of = block_levels(rng, shape, split, -0.22, 0.18) if split else 1.0
    values = jax.random.normal(rng, shape, jnp.float32) * width * factor_of
    return jnp.minimum(jnp.maximum(values, -reach), reach).astype(held_as)


def setup_inputs(seed: int = 0) -> dict:
    seeds = jax.random.split(jax.random.key(seed), 8)
    fwd_state = noise(seeds[0], (3, GROUPS, NX, NY), 1.0, 6.0, ((1, 32), (2, 8), (3, 2)), jnp.float32)
    adj_state = noise(seeds[1], (3, GROUPS, NX, NY), 1.0, 6.0, ((1, 32), (2, 8), (3, 2)), jnp.float32)
    courant = jnp.clip(0.2 + 0.24999999 * jax.random.uniform(seeds[2], (NX, NY), jnp.float32) ** block_levels(seeds[2], (NX, NY), ((0, 8), (1, 2)), -0.2, 0.2), 0.2, 0.45)
    decay_rate = jnp.clip(0.2 + 0.7 * jax.random.uniform(seeds[3], (NX, NY), jnp.float32) ** block_levels(seeds[3], (NX, NY), ((0, 8), (1, 2)), -0.2, 0.2), 0.2, 0.9)
    strength = jnp.clip(0.05 + 0.35 * jax.random.uniform(seeds[4], (NX, NY), jnp.float32) ** block_levels(seeds[4], (NX, NY), ((0, 8), (1, 2)), -0.2, 0.2), 0.05, 0.4)
    footprint = different_ones(seeds[5], GROUPS * N_VX * N_VY, NB, FP, 4096).reshape((GROUPS, N_VX, N_VY, FP))
    owner_map = jax.vmap(lambda own: jax.random.permutation(own, NB))(jax.random.split(seeds[6], N_VX * N_VY)).reshape((N_VX, N_VY, NB)).astype(jnp.int32)
    return dict(fwd_state=fwd_state, adj_state=adj_state, courant=courant, decay_rate=decay_rate, strength=strength, footprint=footprint, owner_map=owner_map)


def laplace(field):
    padded = jnp.pad(field, 1)
    return padded[2:, 1:-1] + padded[:-2, 1:-1] + padded[1:-1, 2:] + padded[1:-1, :-2] - 4.0 * field


def keep_all(field):
    return field


def advance(state, courant, decay_rate, strength, laplace_fn):
    former, current, memory = state
    curve = laplace_fn(current)
    memory = decay_rate * memory + strength * curve
    following = 2.0 * current - former + courant * (curve - memory)
    return (current, following, memory)


def propagate(state, courant, decay_rate, strength, laplace_fn, crop):
    levels = [crop(state[0]), crop(state[1])]
    for number in range(STEPS):
        state = advance(state, courant, decay_rate, strength, laplace_fn)
        levels.append(crop(state[1]))
    return levels


def imaging(forward, adjoint, scale):
    result = None
    for level in range(1, STEPS + 1):
        second = forward[level + 1] - 2.0 * forward[level] + forward[level - 1]
        term = adjoint[STEPS + 2 - level] * second
        result = term if result is None else result + term
    return result * scale


def reference(fwd_state, adj_state, courant, decay_rate, strength, footprint, owner_map):
    scale = 1.0 / GROUPS
    block_ids = jnp.arange(NB, dtype=jnp.int32)

    def per_group(total, inputs):
        forward_in, adjoint_in, listed = inputs
        forward = propagate((forward_in[0], forward_in[1], forward_in[2]), courant, decay_rate, strength, laplace, keep_all)
        adjoint = propagate((adjoint_in[0], adjoint_in[1], adjoint_in[2]), courant, decay_rate, strength, laplace, keep_all)
        gradient = imaging(forward, adjoint, scale)
        tiled = gradient.reshape(N_VX, BX, BR, N_VY, BY, BC).transpose(0, 3, 1, 4, 2, 5).reshape(N_VX, N_VY, NB, BR, BC)
        hits = jnp.any(listed[:, :, :, None] == block_ids, axis=2).astype(jnp.float32)
        return total + tiled * hits[:, :, :, None, None], forward[STEPS + 1]

    start = jnp.zeros((N_VX, N_VY, NB, BR, BC), jnp.float32)
    total, pressure = lax.scan(per_group, start, (jnp.moveaxis(fwd_state, 1, 0), jnp.moveaxis(adj_state, 1, 0), footprint))
    slots = jnp.take_along_axis(total, owner_map[:, :, :, None, None], axis=2)
    gradient_out = slots.transpose(2, 0, 3, 1, 4).reshape(NB, N_VX * BR, N_VY * BC)
    return gradient_out, pressure
```

```python
import jax
import jax.numpy as jnp
from jax import lax
from jax.experimental import pallas as pl
from jax.experimental.pallas import tpu as pltpu
from jax.sharding import PartitionSpec as P

BR = 16
BC = 128
STEPS = 4
HALO = 4
SUB = 8
LANES = 128
FIELDS = 9
TILE_AT = 2 * SUB
VMEM_LIMIT = 48 * 1024 * 1024


def pack_kernel(fwd, adj, courant, decay, strength, side_out, top_out, low_out, cols, tops, lows, sem):
    rows = courant.shape[0]
    vy = lax.axis_index("vy")
    edge = pl.ds(pl.multiple_of((1 - vy) * LANES, LANES), LANES)
    copies = []
    for number, state in enumerate((fwd, adj)):
        at = pl.ds(3 * number, 3)
        copies.append((state.at[:, 0, :, edge], cols.at[at]))
        copies.append((state.at[:, 0, pl.ds(0, SUB), :], tops.at[at]))
        copies.append((state.at[:, 0, pl.ds(rows - SUB, SUB), :], lows.at[at]))
    for number, field in enumerate((courant, decay, strength)):
        copies.append((field.at[:, edge], cols.at[6 + number]))
        copies.append((field.at[pl.ds(0, SUB), :], tops.at[6 + number]))
        copies.append((field.at[pl.ds(rows - SUB, SUB), :], lows.at[6 + number]))
    started = [pltpu.make_async_copy(src, dst, sem.at[n]) for n, (src, dst) in enumerate(copies)]
    for copy in started:
        copy.start()
    for copy in started:
        copy.wait()
    lane = lax.broadcasted_iota(jnp.int32, (SUB, LANES), 1)

    def chunk(number, carry):
        at = pl.ds(pl.multiple_of(number * SUB, SUB), SUB)
        packed = jnp.zeros((SUB, LANES), jnp.float32)
        for field in range(FIELDS):
            moved = pltpu.roll(cols[field, at, :], HALO * field + HALO * (1 - vy), 1)
            here = (lane >= HALO * field) & (lane < HALO * (field + 1))
            packed = jnp.where(here, moved, packed)
        side_out[at, :] = packed
        return carry

    lax.fori_loop(0, rows // SUB, chunk, 0)
    for out, edges, first in ((top_out, tops, 0), (low_out, lows, SUB - HALO)):
        for field in range(FIELDS):
            out[HALO * field : HALO * (field + 1), :] = edges[field, first : first + HALO, :]
        out[HALO * FIELDS : HALO * (FIELDS + 1), :] = jnp.zeros((HALO, 2 * LANES), jnp.float32)


def pack(fwd_state, adj_state, courant, decay_rate, strength):
    rows, columns = courant.shape
    edge = jax.ShapeDtypeStruct((HALO * (FIELDS + 1), columns), jnp.float32)
    return pl.pallas_call(
        pack_kernel,
        out_shape=(jax.ShapeDtypeStruct((rows, LANES), jnp.float32), edge, edge),
        in_specs=[pl.BlockSpec(memory_space=pl.ANY)] * 5,
        out_specs=[pl.BlockSpec(memory_space=pltpu.VMEM)] * 3,
        scratch_shapes=[
            pltpu.VMEM((FIELDS, rows, LANES), jnp.float32),
            pltpu.VMEM((FIELDS, SUB, columns), jnp.float32),
            pltpu.VMEM((FIELDS, SUB, columns), jnp.float32),
            pltpu.SemaphoreType.DMA((15,)),
        ],
        compiler_params=pltpu.CompilerParams(vmem_limit_bytes=VMEM_LIMIT),
        cost_estimate=pl.CostEstimate(flops=600000, bytes_accessed=1500000, transcendentals=0),
        name="pack",
    )(fwd_state, adj_state, courant, decay_rate, strength)


def steps_kernel(
    scale, fwd, adj, courant, decay, strength, side, above, below, footprint, owner,
    ordered, pressure, held, fore, back, curves, partial, slot_of, gain_of, sem,
):
    rows = courant.shape[0]
    chunks = rows // SUB
    vy = lax.axis_index("vy")
    copies = []
    for half in range(2):
        columns = pl.ds(half * LANES, LANES)
        for number, state in enumerate((fwd, adj)):
            copies.append((state.at[:, 0, :, columns], held.at[pl.ds(3 * number, 3), half, pl.ds(TILE_AT, rows), :]))
        for number, field in enumerate((courant, decay, strength)):
            copies.append((field.at[:, columns], held.at[6 + number, half, pl.ds(TILE_AT, rows), :]))
    started = [pltpu.make_async_copy(src, dst, sem.at[n]) for n, (src, dst) in enumerate(copies)]
    for copy in started:
        copy.start()

    lane = lax.broadcasted_iota(jnp.int32, (SUB, LANES), 1)
    sub = lax.broadcasted_iota(jnp.int32, (SUB, LANES), 0)
    beside = (lane >= (LANES - HALO) * vy) & (lane < (LANES - HALO) * vy + HALO)
    zero = jnp.zeros((SUB, LANES), jnp.float32)
    first, last = sub == 0, sub == SUB - 1
    lane_first, lane_last = lane == 0, lane == LANES - 1

    def spread(strip, field):
        shift = lax.rem(LANES - HALO * field + (LANES - HALO) * vy, LANES)
        return jnp.where(beside, pltpu.roll(strip, shift, 1), zero)

    def clear(number, carry):
        gain_of[number] = jnp.float32(0.0)
        return carry

    lax.fori_loop(0, gain_of.shape[0], clear, 0)

    def list_block(number, carry):
        gain_of[footprint[number]] = jnp.float32(scale)
        return carry

    lax.fori_loop(0, footprint.shape[0], list_block, 0)

    def place(number, carry):
        slot_of[owner[number]] = number
        return carry

    lax.fori_loop(0, owner.shape[0], place, 0)

    for buffers in (held, fore, back):
        for field in range(buffers.shape[0]):
            for part in range(3):
                buffers[field, part, 0:SUB, :] = zero
                buffers[field, part, rows + 3 * SUB : rows + 4 * SUB, :] = zero
    corner_above = above[HALO * (FIELDS - 1) : HALO * (FIELDS + 1), 0:LANES]
    corner_below = pltpu.roll(below[HALO * (FIELDS - 1) : HALO * (FIELDS + 1), 0:LANES], HALO, 0)
    upper, lower = sub >= HALO, sub < HALO
    for field in range(FIELDS):
        at = (field // 2) * SUB
        for half in range(2):
            columns = slice(half * LANES, (half + 1) * LANES)
            value = above[at : at + SUB, columns]
            if field % 2 == 0:
                value = pltpu.roll(value, HALO, 0)
            held[field, half, SUB : 2 * SUB, :] = jnp.where(upper, value, zero)
            value = below[at : at + SUB, columns]
            if field % 2 == 1:
                value = pltpu.roll(value, HALO, 0)
            held[field, half, rows + 2 * SUB : rows + 3 * SUB, :] = jnp.where(lower, value, zero)
        held[field, 2, SUB : 2 * SUB, :] = jnp.where(upper, spread(corner_above, field), zero)
        held[field, 2, rows + 2 * SUB : rows + 3 * SUB, :] = jnp.where(lower, spread(corner_below, field), zero)

    def beside_tile(number, carry):
        strip = side[pl.ds(pl.multiple_of(number * SUB, SUB), SUB), :]
        at = pl.ds(pl.multiple_of(number * SUB + TILE_AT, SUB), SUB)
        for field in range(FIELDS):
            held[field, 2, at, :] = spread(strip, field)
        return carry

    lax.fori_loop(0, chunks, beside_tile, 0)
    for copy in started:
        copy.wait()

    def laplace(buffers, level, at):
        before = pl.ds(pl.multiple_of(at - SUB, SUB), SUB)
        now = pl.ds(pl.multiple_of(at, SUB), SUB)
        after = pl.ds(pl.multiple_of(at + SUB, SUB), SUB)
        centre = [buffers[level, part, now, :] for part in range(3)]
        right = [pltpu.roll(value, LANES - 1, 1) for value in centre]
        left = [pltpu.roll(value, 1, 1) for value in centre]
        result = []
        for part in range(3):
            up = jnp.where(first, pltpu.roll(buffers[level, part, before, :], 1, 0), pltpu.roll(centre[part], 1, 0))
            down = jnp.where(
                last, pltpu.roll(buffers[level, part, after, :], SUB - 1, 0), pltpu.roll(centre[part], SUB - 1, 0)
            )
            west = jnp.where(lane_first, left[(part + 2) % 3], left[part])
            east = jnp.where(lane_last, right[(part + 1) % 3], right[part])
            result.append((down + up) + (east + west) - 4.0 * centre[part])
        return centre, result

    def level_of(own, base, step):
        if step == 1:
            return held, base, held, base + 1
        if step == 2:
            return held, base + 1, own, 0
        return own, step - 3, own, step - 2

    for step in range(1, STEPS + 1):
        final = step == STEPS

        def advance(number, carry, step=step, final=final):
            at = number * SUB + (TILE_AT if final else SUB)
            now = pl.ds(pl.multiple_of(at, SUB), SUB)
            speed = [held[6, part, now, :] for part in range(3)]
            keep = [held[7, part, now, :] for part in range(3)]
            loss = [held[8, part, now, :] for part in range(3)]
            parts = range(2) if final else range(3)
            found = []
            for own, base in ((fore, 0), (back, 3)):
                old, old_at, new, new_at = level_of(own, base, step)
                centre, curve = laplace(new, new_at, at)
                seconds, nexts = [], []
                for part in parts:
                    memory = keep[part] * held[base + 2, part, now, :] + loss[part] * curve[part]
                    second = speed[part] * (curve[part] - memory)
                    following = 2.0 * centre[part] - old[old_at, part, now, :] + second
                    if not final:
                        held[base + 2, part, now, :] = memory
                        own[step - 1, part, now, :] = following
                    seconds.append(second)
                    nexts.append(following)
                found.append((seconds, nexts))
            seconds, nexts = found[0]
            adjoint = found[1][1]
            for part in range(2):
                if step <= 2:
                    curves[step - 1, part, now, :] = seconds[part]
                elif step == 3:
                    partial[part, now, :] = seconds[part] * back[1, part, now, :] + curves[1, part, now, :] * adjoint[part]
                else:
                    total = partial[part, now, :] + (
                        seconds[part] * back[0, part, now, :] + curves[0, part, now, :] * adjoint[part]
                    )
                    block = (number // 2) * 2 + part
                    inside = pl.ds(pl.multiple_of(lax.rem(number, 2) * SUB, SUB), SUB)
                    ordered[slot_of[block], inside, :] = total * gain_of[block]
                    tile = pl.ds(pl.multiple_of(number * SUB, SUB), SUB)
                    pressure[0, tile, part * LANES : (part + 1) * LANES] = nexts[part]
            return carry

        lax.fori_loop(0, chunks if final else chunks + 2, advance, 0)


def run_steps(scale, fwd_state, adj_state, courant, decay_rate, strength, side, above, below, footprint, owner_map):
    rows, columns = courant.shape
    blocks = owner_map.shape[0]
    extended = (3, rows + 4 * SUB, LANES)
    return pl.pallas_call(
        lambda *refs: steps_kernel(scale, *refs),
        out_shape=(
            jax.ShapeDtypeStruct((blocks, BR, BC), jnp.float32),
            jax.ShapeDtypeStruct((1, rows, columns), jnp.float32),
        ),
        in_specs=[pl.BlockSpec(memory_space=pl.ANY)] * 5
        + [pl.BlockSpec(memory_space=pltpu.VMEM)] * 3
        + [pl.BlockSpec(memory_space=pltpu.SMEM)] * 2,
        out_specs=[pl.BlockSpec(memory_space=pltpu.VMEM)] * 2,
        scratch_shapes=[
            pltpu.VMEM((FIELDS,) + extended, jnp.float32),
            pltpu.VMEM((STEPS - 1,) + extended, jnp.float32),
            pltpu.VMEM((STEPS - 1,) + extended, jnp.float32),
            pltpu.VMEM((2,) + extended, jnp.float32),
            pltpu.VMEM(extended, jnp.float32),
            pltpu.SMEM((blocks,), jnp.int32),
            pltpu.SMEM((blocks,), jnp.float32),
            pltpu.SemaphoreType.DMA((10,)),
        ],
        compiler_params=pltpu.CompilerParams(vmem_limit_bytes=VMEM_LIMIT),
        cost_estimate=pl.CostEstimate(flops=14000000, bytes_accessed=2900000, transcendentals=0),
        name="steps",
    )(fwd_state, adj_state, courant, decay_rate, strength, side, above, below, footprint, owner_map)


def shards(fwd_state, adj_state, courant, decay_rate, strength, footprint, owner_map):
    groups = lax.axis_size("emit")
    tiles = lax.axis_size("vx")
    rows = courant.shape[0]
    fields = (fwd_state, adj_state, courant, decay_rate, strength)
    side, top, low = pack(*fields)
    side = lax.ppermute(side, "vy", [(0, 1), (1, 0)])
    corners = (HALO * FIELDS, 0)
    top = lax.dynamic_update_slice(top, side[:HALO], corners)
    low = lax.dynamic_update_slice(low, side[rows - HALO :], corners)
    below = lax.ppermute(top, "vx", [(i + 1, i) for i in range(tiles - 1)])
    above = lax.ppermute(low, "vx", [(i, i + 1) for i in range(tiles - 1)])
    ordered, pressure = run_steps(
        1.0 / groups, *fields, side, above, below, footprint.reshape(-1), owner_map.reshape(-1)
    )
    sent = lax.all_to_all(ordered, "emit", 0, 0, tiled=True)
    gradient = jnp.sum(sent.reshape(groups, -1, BR, BC), axis=0)
    return gradient, pressure


def solution(mesh):
    in_specs = (
        P(None, "emit", "vx", "vy"),
        P(None, "emit", "vx", "vy"),
        P("vx", "vy"),
        P("vx", "vy"),
        P("vx", "vy"),
        P("emit", "vx", "vy", None),
        P("vx", "vy", None),
    )
    out_specs = (P("emit", "vx", "vy"), P("emit", "vx", "vy"))
    return jax.shard_map(shards, mesh=mesh, in_specs=in_specs, out_specs=out_specs, check_vma=False)
```

```python
import jax
import jax.numpy as jnp
from jax import lax
from jax.experimental import pallas as pl
from jax.experimental.pallas import tpu as pltpu
from jax.sharding import PartitionSpec as P

BR = 16
BC = 128
STEPS = 4
HALO = 4
SUB = 8
LANES = 128
FIELDS = 9
TILE_AT = 2 * SUB
VMEM_LIMIT = 48 * 1024 * 1024
GROUP = (13, 37, 35, 33)


def pack_kernel(fwd, adj, courant, decay, strength, side_out, top_out, low_out, cols, tops, lows, sem):
    rows = courant.shape[0]
    vy = lax.axis_index("vy")
    edge = pl.ds(pl.multiple_of((1 - vy) * LANES, LANES), LANES)
    copies = []
    for number, state in enumerate((fwd, adj)):
        at = pl.ds(3 * number, 3)
        copies.append((state.at[:, 0, :, edge], cols.at[at]))
        copies.append((state.at[:, 0, pl.ds(0, SUB), :], tops.at[at]))
        copies.append((state.at[:, 0, pl.ds(rows - SUB, SUB), :], lows.at[at]))
    for number, field in enumerate((courant, decay, strength)):
        copies.append((field.at[:, edge], cols.at[6 + number]))
        copies.append((field.at[pl.ds(0, SUB), :], tops.at[6 + number]))
        copies.append((field.at[pl.ds(rows - SUB, SUB), :], lows.at[6 + number]))
    started = [pltpu.make_async_copy(src, dst, sem.at[n]) for n, (src, dst) in enumerate(copies)]
    for copy in started:
        copy.start()
    for copy in started:
        copy.wait()
    lane = lax.broadcasted_iota(jnp.int32, (SUB, LANES), 1)

    for at in range(0, rows, SUB):
        packed = jnp.zeros((SUB, LANES), jnp.float32)
        for field in range(FIELDS):
            moved = pltpu.roll(cols[field, at : at + SUB, :], HALO * field + HALO * (1 - vy), 1)
            here = (lane >= HALO * field) & (lane < HALO * (field + 1))
            packed = jnp.where(here, moved, packed)
        side_out[at : at + SUB, :] = packed
    for out, edges, first in ((top_out, tops, 0), (low_out, lows, SUB - HALO)):
        for field in range(FIELDS):
            out[HALO * field : HALO * (field + 1), :] = edges[field, first : first + HALO, :]
        out[HALO * FIELDS : HALO * (FIELDS + 1), :] = jnp.zeros((HALO, 2 * LANES), jnp.float32)


def pack(fwd_state, adj_state, courant, decay_rate, strength):
    rows, columns = courant.shape
    edge = jax.ShapeDtypeStruct((HALO * (FIELDS + 1), columns), jnp.float32)
    return pl.pallas_call(
        pack_kernel,
        out_shape=(jax.ShapeDtypeStruct((rows, LANES), jnp.float32), edge, edge),
        in_specs=[pl.BlockSpec(memory_space=pltpu.HBM)] * 5,
        out_specs=[pl.BlockSpec(memory_space=pltpu.VMEM)] * 3,
        scratch_shapes=[
            pltpu.VMEM((FIELDS, rows, LANES), jnp.float32),
            pltpu.VMEM((FIELDS, SUB, columns), jnp.float32),
            pltpu.VMEM((FIELDS, SUB, columns), jnp.float32),
            pltpu.SemaphoreType.DMA((15,)),
        ],
        compiler_params=pltpu.CompilerParams(vmem_limit_bytes=VMEM_LIMIT),
        cost_estimate=pl.CostEstimate(flops=600000, bytes_accessed=1500000, transcendentals=0),
        name="pack",
    )(fwd_state, adj_state, courant, decay_rate, strength)


def steps_kernel(
    scale, fwd, adj, courant, decay, strength, side, above, below, footprint, owner,
    ordered, pressure, held, coefs, starts, memories, fore, back, curves, partial, found_g, found_p,
    slot_of, gain_of, sem, out_sem,
):
    rows = courant.shape[0]
    vy = lax.axis_index("vy")
    copies = []
    for half in range(2):
        columns = pl.ds(half * LANES, LANES)
        for number, state in enumerate((fwd, adj)):
            copies.append((state.at[:, 0, :, columns], held.at[pl.ds(3 * number, 3), half, pl.ds(TILE_AT, rows), :]))
        for number, field in enumerate((courant, decay, strength)):
            copies.append((field.at[:, columns], held.at[6 + number, half, pl.ds(TILE_AT, rows), :]))
    started = [pltpu.make_async_copy(src, dst, sem.at[n]) for n, (src, dst) in enumerate(copies)]
    for copy in started:
        copy.start()

    lane = lax.broadcasted_iota(jnp.int32, (SUB, LANES), 1)
    sub = lax.broadcasted_iota(jnp.int32, (SUB, LANES), 0)
    beside = (lane >= (LANES - HALO) * vy) & (lane < (LANES - HALO) * vy + HALO)
    zero = jnp.zeros((SUB, LANES), jnp.float32)
    lane_first, lane_last = lane == 0, lane == LANES - 1

    def spread(strip, field):
        shift = lax.rem(LANES - HALO * field + (LANES - HALO) * vy, LANES)
        return jnp.where(beside, pltpu.roll(strip, shift, 1), zero)

    for block in range(gain_of.shape[0]):
        gain_of[block] = jnp.float32(0.0)
    for number in range(footprint.shape[0]):
        gain_of[footprint[number]] = jnp.float32(scale)
    for number in range(owner.shape[0]):
        slot_of[owner[number]] = number

    corner_above = above[HALO * (FIELDS - 1) : HALO * (FIELDS + 1), 0:LANES]
    corner_below = pltpu.roll(below[HALO * (FIELDS - 1) : HALO * (FIELDS + 1), 0:LANES], HALO, 0)
    upper, lower = sub >= HALO, sub < HALO
    for field in range(FIELDS):
        at = (field // 2) * SUB
        for half in range(2):
            columns = slice(half * LANES, (half + 1) * LANES)
            value = above[at : at + SUB, columns]
            if field % 2 == 0:
                value = pltpu.roll(value, HALO, 0)
            held[field, half, SUB : 2 * SUB, :] = jnp.where(upper, value, zero)
            value = below[at : at + SUB, columns]
            if field % 2 == 1:
                value = pltpu.roll(value, HALO, 0)
            held[field, half, rows + 2 * SUB : rows + 3 * SUB, :] = jnp.where(lower, value, zero)
        held[field, 2, SUB : 2 * SUB, :] = jnp.where(upper, spread(corner_above, field), zero)
        held[field, 2, rows + 2 * SUB : rows + 3 * SUB, :] = jnp.where(lower, spread(corner_below, field), zero)
    for at in range(0, rows, SUB):
        strip = side[at : at + SUB, :]
        for field in range(FIELDS):
            held[field, 2, TILE_AT + at : TILE_AT + at + SUB, :] = spread(strip, field)
    for copy in started:
        copy.wait()

    pitch = rows // SUB + 1

    def strips(field, part, t):
        return held[field, part, pl.ds(TILE_AT - HALO + t, SUB, stride=pitch), :]

    def advance(step, base_t, group):
        final = step == STEPS
        parts = range(2) if final else range(3)
        ts = [base_t + g for g in range(group)]
        stores = []
        speed, keep, loss = {}, {}, {}
        for part in parts:
            for g, t in enumerate(ts):
                for number, of in enumerate((speed, keep, loss)):
                    if step == 1:
                        of[part, g] = strips(6 + number, part, t)
                        stores.append((coefs, (number, part, SUB + t), of[part, g]))
                    else:
                        of[part, g] = coefs[number, part, SUB + t]
        results = []
        for own, state in ((fore, 0), (back, 1)):

            def level(number, part, t, own=own, state=state):
                if number >= 2:
                    return own[number - 2, part, SUB + t]
                if step == 1:
                    return strips(3 * state + number, part, t)
                return starts[state, part, SUB + t]

            centre = {
                (part, g): level(step, part, base_t + g)
                for part in range(3)
                for g in range(-1, group + 1)
                if part in parts or 0 <= g < group
            }
            seconds, nexts = {}, {}
            for g, t in enumerate(ts):
                right = [pltpu.roll(centre[part, g], LANES - 1, 1) for part in range(3)]
                left = [pltpu.roll(centre[part, g], 1, 1) for part in range(3)]
                for part in parts:
                    west = jnp.where(lane_first, left[(part + 2) % 3], left[part])
                    east = jnp.where(lane_last, right[(part + 1) % 3], right[part])
                    now = centre[part, g]
                    curve = (centre[part, g - 1] + centre[part, g + 1]) + (east + west) - 4.0 * now
                    memory = strips(3 * state + 2, part, t) if step == 1 else memories[state, part, SUB + t]
                    memory = keep[part, g] * memory + loss[part, g] * curve
                    second = speed[part, g] * (curve - memory)
                    following = 2.0 * now - level(step - 1, part, t) + second
                    if step == 1:
                        stores.append((starts, (state, part, SUB + t), now))
                    if not final:
                        stores.append((memories, (state, part, SUB + t), memory))
                        stores.append((own, (step - 1, part, SUB + t), following))
                    seconds[part, g] = second
                    nexts[part, g] = following
            results.append((seconds, nexts))
        (seconds, nexts), (_, adjoint) = results
        for part in range(2):
            for g, t in enumerate(ts):
                if step <= 2:
                    stores.append((curves, (step - 1, part, SUB + t), seconds[part, g]))
                    continue
                other = 4 - step
                value = (
                    seconds[part, g] * back[other, part, SUB + t] + curves[other, part, SUB + t] * adjoint[part, g]
                )
                if step == 3:
                    stores.append((partial, (part, SUB + t), value))
                else:
                    rows_at = pl.ds(HALO + t, SUB, stride=pitch)
                    stores.append((found_g, (part, rows_at), partial[part, SUB + t] + value))
                    stores.append((found_p, (part, rows_at), nexts[part, g]))
        for ref, index, value in stores:
            ref[index] = value

    for step in range(1, STEPS + 1):
        margin = STEPS - step
        count = pitch + 2 * margin
        group = GROUP[step - 1]
        if count == group:
            advance(step, -margin, group)
        else:

            def turn(number, carry, step=step, margin=margin, group=group):
                advance(step, number * group - margin, group)
                return carry

            lax.fori_loop(0, count // group, turn, 0)

    leaving = [
        pltpu.make_async_copy(
            found_p.at[half, pl.ds(SUB, rows), :], pressure.at[0, :, pl.ds(half * LANES, LANES)], out_sem.at[half]
        )
        for half in range(2)
    ]
    for copy in leaving:
        copy.start()
    for block in range(gain_of.shape[0]):
        at = SUB + (block // 2) * BR
        ordered[slot_of[block]] = found_g[block % 2, at : at + BR, :] * gain_of[block]
    for copy in leaving:
        copy.wait()


def run_steps(scale, fwd_state, adj_state, courant, decay_rate, strength, side, above, below, footprint, owner_map):
    rows, columns = courant.shape
    blocks = owner_map.shape[0]
    strip = (3, rows // SUB + 16, SUB, LANES)
    found = (2, rows + 6 * SUB, LANES)
    return pl.pallas_call(
        lambda *refs: steps_kernel(scale, *refs),
        out_shape=(
            jax.ShapeDtypeStruct((blocks, BR, BC), jnp.float32),
            jax.ShapeDtypeStruct((1, rows, columns), jnp.float32),
        ),
        in_specs=[pl.BlockSpec(memory_space=pltpu.HBM)] * 5
        + [pl.BlockSpec(memory_space=pltpu.VMEM)] * 3
        + [pl.BlockSpec(memory_space=pltpu.SMEM)] * 2,
        out_specs=[pl.BlockSpec(memory_space=pltpu.VMEM), pl.BlockSpec(memory_space=pltpu.HBM)],
        scratch_shapes=[
            pltpu.VMEM((FIELDS, 3, rows + 7 * SUB, LANES), jnp.float32),
            pltpu.VMEM((3,) + strip, jnp.float32),
            pltpu.VMEM((2,) + strip, jnp.float32),
            pltpu.VMEM((2,) + strip, jnp.float32),
            pltpu.VMEM((STEPS - 1,) + strip, jnp.float32),
            pltpu.VMEM((STEPS - 1,) + strip, jnp.float32),
            pltpu.VMEM((2,) + strip, jnp.float32),
            pltpu.VMEM(strip, jnp.float32),
            pltpu.VMEM(found, jnp.float32),
            pltpu.VMEM(found, jnp.float32),
            pltpu.SMEM((blocks,), jnp.int32),
            pltpu.SMEM((blocks,), jnp.float32),
            pltpu.SemaphoreType.DMA((10,)),
            pltpu.SemaphoreType.DMA((2,)),
        ],
        compiler_params=pltpu.CompilerParams(vmem_limit_bytes=VMEM_LIMIT),
        cost_estimate=pl.CostEstimate(flops=14000000, bytes_accessed=2900000, transcendentals=0),
        name="steps",
    )(fwd_state, adj_state, courant, decay_rate, strength, side, above, below, footprint, owner_map)


def shards(fwd_state, adj_state, courant, decay_rate, strength, footprint, owner_map):
    groups = lax.axis_size("emit")
    tiles = lax.axis_size("vx")
    rows = courant.shape[0]
    fields = (fwd_state, adj_state, courant, decay_rate, strength)
    side, top, low = pack(*fields)
    side = lax.ppermute(side, "vy", [(0, 1), (1, 0)])
    corners = (HALO * FIELDS, 0)
    top = lax.dynamic_update_slice(top, side[:HALO], corners)
    low = lax.dynamic_update_slice(low, side[rows - HALO :], corners)
    below = lax.ppermute(top, "vx", [(i + 1, i) for i in range(tiles - 1)])
    above = lax.ppermute(low, "vx", [(i, i + 1) for i in range(tiles - 1)])
    ordered, pressure = run_steps(
        1.0 / groups, *fields, side, above, below, footprint.reshape(-1), owner_map.reshape(-1)
    )
    sent = lax.all_to_all(ordered, "emit", 0, 0, tiled=True)
    gradient = jnp.sum(sent.reshape(groups, -1, BR, BC), axis=0)
    return gradient, pressure


def solution(mesh):
    in_specs = (
        P(None, "emit", "vx", "vy"),
        P(None, "emit", "vx", "vy"),
        P("vx", "vy"),
        P("vx", "vy"),
        P("vx", "vy"),
        P("emit", "vx", "vy", None),
        P("vx", "vy", None),
    )
    out_specs = (P("emit", "vx", "vy"), P("emit", "vx", "vy"))
    return jax.shard_map(shards, mesh=mesh, in_specs=in_specs, out_specs=out_specs, check_vma=False)
```

```python
import jax
import jax.numpy as jnp
from jax import lax
from jax.experimental import pallas as pl
from jax.experimental.pallas import tpu as pltpu
from jax.sharding import PartitionSpec as P

BR = 16
BC = 128
STEPS = 4
HALO = 4
SUB = 8
LANES = 128
FIELDS = 9
TILE_AT = 2 * SUB
VMEM_LIMIT = 48 * 1024 * 1024
GROUP = (13, 37, 35, 33)


def in_hbm(array):
    return pltpu.with_memory_space_constraint(array, pltpu.HBM)


def pack_kernel(fwd, adj, courant, decay, strength, side_out, top_out, low_out, cols, tops, lows, sem):
    rows = courant.shape[0]
    vy = lax.axis_index("vy")
    edge = pl.ds(pl.multiple_of((1 - vy) * LANES, LANES), LANES)
    copies = []
    for number, state in enumerate((fwd, adj)):
        at = pl.ds(3 * number, 3)
        copies.append((state.at[:, 0, :, edge], cols.at[at]))
        copies.append((state.at[:, 0, pl.ds(0, SUB), :], tops.at[at]))
        copies.append((state.at[:, 0, pl.ds(rows - SUB, SUB), :], lows.at[at]))
    for number, field in enumerate((courant, decay, strength)):
        copies.append((field.at[:, edge], cols.at[6 + number]))
        copies.append((field.at[pl.ds(0, SUB), :], tops.at[6 + number]))
        copies.append((field.at[pl.ds(rows - SUB, SUB), :], lows.at[6 + number]))
    started = [pltpu.make_async_copy(src, dst, sem.at[n]) for n, (src, dst) in enumerate(copies)]
    for copy in started:
        copy.start()
    for copy in started:
        copy.wait()
    lane = lax.broadcasted_iota(jnp.int32, (SUB, LANES), 1)

    for at in range(0, rows, SUB):
        packed = jnp.zeros((SUB, LANES), jnp.float32)
        for field in range(FIELDS):
            moved = pltpu.roll(cols[field, at : at + SUB, :], HALO * field + HALO * (1 - vy), 1)
            here = (lane >= HALO * field) & (lane < HALO * (field + 1))
            packed = jnp.where(here, moved, packed)
        side_out[at : at + SUB, :] = packed
    for out, edges, first in ((top_out, tops, 0), (low_out, lows, SUB - HALO)):
        for field in range(FIELDS):
            out[HALO * field : HALO * (field + 1), :] = edges[field, first : first + HALO, :]
        out[HALO * FIELDS : HALO * (FIELDS + 1), :] = jnp.zeros((HALO, 2 * LANES), jnp.float32)


def pack(fwd_state, adj_state, courant, decay_rate, strength):
    rows, columns = courant.shape
    edge = jax.ShapeDtypeStruct((HALO * (FIELDS + 1), columns), jnp.float32)
    return pl.pallas_call(
        pack_kernel,
        out_shape=(jax.ShapeDtypeStruct((rows, LANES), jnp.float32), edge, edge),
        in_specs=[pl.BlockSpec(memory_space=pltpu.HBM)] * 5,
        out_specs=[pl.BlockSpec(memory_space=pltpu.VMEM)] * 3,
        scratch_shapes=[
            pltpu.VMEM((FIELDS, rows, LANES), jnp.float32),
            pltpu.VMEM((FIELDS, SUB, columns), jnp.float32),
            pltpu.VMEM((FIELDS, SUB, columns), jnp.float32),
            pltpu.SemaphoreType.DMA((15,)),
        ],
        compiler_params=pltpu.CompilerParams(vmem_limit_bytes=VMEM_LIMIT),
        cost_estimate=pl.CostEstimate(flops=600000, bytes_accessed=1500000, transcendentals=0),
        name="pack",
    )(fwd_state, adj_state, courant, decay_rate, strength)


def steps_kernel(
    scale, fwd, adj, courant, decay, strength, side, above, below, footprint_in, owner_in,
    ordered, pressure, held, coefs, starts, memories, fore, back, curves, partial, found_g, found_p,
    footprint, owner, slot_of, gain_of, sem, list_sem, out_sem,
):
    rows = courant.shape[0]
    vy = lax.axis_index("vy")
    copies = []
    for half in range(2):
        columns = pl.ds(half * LANES, LANES)
        for number, state in enumerate((fwd, adj)):
            copies.append((state.at[:, 0, :, columns], held.at[pl.ds(3 * number, 3), half, pl.ds(TILE_AT, rows), :]))
        for number, field in enumerate((courant, decay, strength)):
            copies.append((field.at[:, columns], held.at[6 + number, half, pl.ds(TILE_AT, rows), :]))
    started = [pltpu.make_async_copy(src, dst, sem.at[n]) for n, (src, dst) in enumerate(copies)]
    for copy in started:
        copy.start()
    lists = [
        pltpu.make_async_copy(footprint_in, footprint, list_sem.at[0]),
        pltpu.make_async_copy(owner_in, owner, list_sem.at[1]),
    ]
    for copy in lists:
        copy.start()

    lane = lax.broadcasted_iota(jnp.int32, (SUB, LANES), 1)
    sub = lax.broadcasted_iota(jnp.int32, (SUB, LANES), 0)
    beside = (lane >= (LANES - HALO) * vy) & (lane < (LANES - HALO) * vy + HALO)
    zero = jnp.zeros((SUB, LANES), jnp.float32)
    lane_first, lane_last = lane == 0, lane == LANES - 1

    def spread(strip, field):
        shift = lax.rem(LANES - HALO * field + (LANES - HALO) * vy, LANES)
        return jnp.where(beside, pltpu.roll(strip, shift, 1), zero)

    corner_above = above[HALO * (FIELDS - 1) : HALO * (FIELDS + 1), 0:LANES]
    corner_below = pltpu.roll(below[HALO * (FIELDS - 1) : HALO * (FIELDS + 1), 0:LANES], HALO, 0)
    upper, lower = sub >= HALO, sub < HALO
    for field in range(FIELDS):
        at = (field // 2) * SUB
        for half in range(2):
            columns = slice(half * LANES, (half + 1) * LANES)
            value = above[at : at + SUB, columns]
            if field % 2 == 0:
                value = pltpu.roll(value, HALO, 0)
            held[field, half, SUB : 2 * SUB, :] = jnp.where(upper, value, zero)
            value = below[at : at + SUB, columns]
            if field % 2 == 1:
                value = pltpu.roll(value, HALO, 0)
            held[field, half, rows + 2 * SUB : rows + 3 * SUB, :] = jnp.where(lower, value, zero)
        held[field, 2, SUB : 2 * SUB, :] = jnp.where(upper, spread(corner_above, field), zero)
        held[field, 2, rows + 2 * SUB : rows + 3 * SUB, :] = jnp.where(lower, spread(corner_below, field), zero)
    for at in range(0, rows, SUB):
        strip = side[at : at + SUB, :]
        for field in range(FIELDS):
            held[field, 2, TILE_AT + at : TILE_AT + at + SUB, :] = spread(strip, field)
    for copy in lists:
        copy.wait()
    for block in range(gain_of.shape[0]):
        gain_of[block] = jnp.float32(0.0)
    for number in range(footprint.shape[0]):
        gain_of[footprint[number]] = jnp.float32(scale)
    for number in range(owner.shape[0]):
        slot_of[owner[number]] = number
    for copy in started:
        copy.wait()

    pitch = rows // SUB + 1

    def strips(field, part, t):
        return held[field, part, pl.ds(TILE_AT - HALO + t, SUB, stride=pitch), :]

    def advance(step, base_t, group):
        final = step == STEPS
        parts = range(2) if final else range(3)
        ts = [base_t + g for g in range(group)]
        stores = []
        speed, keep, loss = {}, {}, {}
        for part in parts:
            for g, t in enumerate(ts):
                for number, of in enumerate((speed, keep, loss)):
                    if step == 1:
                        of[part, g] = strips(6 + number, part, t)
                        stores.append((coefs, (number, part, SUB + t), of[part, g]))
                    else:
                        of[part, g] = coefs[number, part, SUB + t]
        results = []
        for own, state in ((fore, 0), (back, 1)):

            def level(number, part, t, own=own, state=state):
                if number >= 2:
                    return own[number - 2, part, SUB + t]
                if step == 1:
                    return strips(3 * state + number, part, t)
                return starts[state, part, SUB + t]

            centre = {
                (part, g): level(step, part, base_t + g)
                for part in range(3)
                for g in range(-1, group + 1)
                if part in parts or 0 <= g < group
            }
            seconds, nexts = {}, {}
            for g, t in enumerate(ts):
                right = [pltpu.roll(centre[part, g], LANES - 1, 1) for part in range(3)]
                left = [pltpu.roll(centre[part, g], 1, 1) for part in range(3)]
                for part in parts:
                    west = jnp.where(lane_first, left[(part + 2) % 3], left[part])
                    east = jnp.where(lane_last, right[(part + 1) % 3], right[part])
                    now = centre[part, g]
                    curve = (centre[part, g - 1] + centre[part, g + 1]) + (east + west) - 4.0 * now
                    memory = strips(3 * state + 2, part, t) if step == 1 else memories[state, part, SUB + t]
                    memory = keep[part, g] * memory + loss[part, g] * curve
                    second = speed[part, g] * (curve - memory)
                    following = 2.0 * now - level(step - 1, part, t) + second
                    if step == 1:
                        stores.append((starts, (state, part, SUB + t), now))
                    if not final:
                        stores.append((memories, (state, part, SUB + t), memory))
                        stores.append((own, (step - 1, part, SUB + t), following))
                    seconds[part, g] = second
                    nexts[part, g] = following
            results.append((seconds, nexts))
        (seconds, nexts), (_, adjoint) = results
        for part in range(2):
            for g, t in enumerate(ts):
                if step <= 2:
                    stores.append((curves, (step - 1, part, SUB + t), seconds[part, g]))
                    continue
                other = 4 - step
                value = (
                    seconds[part, g] * back[other, part, SUB + t] + curves[other, part, SUB + t] * adjoint[part, g]
                )
                if step == 3:
                    stores.append((partial, (part, SUB + t), value))
                else:
                    rows_at = pl.ds(HALO + t, SUB, stride=pitch)
                    stores.append((found_g, (part, rows_at), partial[part, SUB + t] + value))
                    stores.append((found_p, (part, rows_at), nexts[part, g]))
        for ref, index, value in stores:
            ref[index] = value

    for step in range(1, STEPS + 1):
        margin = STEPS - step
        count = pitch + 2 * margin
        group = GROUP[step - 1]
        if count == group:
            advance(step, -margin, group)
        else:

            def turn(number, carry, step=step, margin=margin, group=group):
                advance(step, number * group - margin, group)
                return carry

            lax.fori_loop(0, count // group, turn, 0)

    leaving = [
        pltpu.make_async_copy(
            found_p.at[half, pl.ds(SUB, rows), :], pressure.at[0, :, pl.ds(half * LANES, LANES)], out_sem.at[half]
        )
        for half in range(2)
    ]
    for copy in leaving:
        copy.start()
    for block in range(gain_of.shape[0]):
        at = SUB + (block // 2) * BR
        ordered[slot_of[block]] = found_g[block % 2, at : at + BR, :] * gain_of[block]
    for copy in leaving:
        copy.wait()


def run_steps(scale, fwd_state, adj_state, courant, decay_rate, strength, side, above, below, footprint, owner_map):
    rows, columns = courant.shape
    blocks = owner_map.shape[0]
    strip = (3, rows // SUB + 16, SUB, LANES)
    found = (2, rows + 6 * SUB, LANES)
    return pl.pallas_call(
        lambda *refs: steps_kernel(scale, *refs),
        out_shape=(
            jax.ShapeDtypeStruct((blocks, BR, BC), jnp.float32),
            jax.ShapeDtypeStruct((1, rows, columns), jnp.float32),
        ),
        in_specs=[pl.BlockSpec(memory_space=pltpu.HBM)] * 5
        + [pl.BlockSpec(memory_space=pltpu.VMEM)] * 3
        + [pl.BlockSpec(memory_space=pltpu.HBM)] * 2,
        out_specs=[pl.BlockSpec(memory_space=pltpu.VMEM), pl.BlockSpec(memory_space=pltpu.HBM)],
        scratch_shapes=[
            pltpu.VMEM((FIELDS, 3, rows + 7 * SUB, LANES), jnp.float32),
            pltpu.VMEM((3,) + strip, jnp.float32),
            pltpu.VMEM((2,) + strip, jnp.float32),
            pltpu.VMEM((2,) + strip, jnp.float32),
            pltpu.VMEM((STEPS - 1,) + strip, jnp.float32),
            pltpu.VMEM((STEPS - 1,) + strip, jnp.float32),
            pltpu.VMEM((2,) + strip, jnp.float32),
            pltpu.VMEM(strip, jnp.float32),
            pltpu.VMEM(found, jnp.float32),
            pltpu.VMEM(found, jnp.float32),
            pltpu.SMEM(footprint.shape, jnp.int32),
            pltpu.SMEM((blocks,), jnp.int32),
            pltpu.SMEM((blocks,), jnp.int32),
            pltpu.SMEM((blocks,), jnp.float32),
            pltpu.SemaphoreType.DMA((10,)),
            pltpu.SemaphoreType.DMA((2,)),
            pltpu.SemaphoreType.DMA((2,)),
        ],
        compiler_params=pltpu.CompilerParams(vmem_limit_bytes=VMEM_LIMIT),
        cost_estimate=pl.CostEstimate(flops=14000000, bytes_accessed=2900000, transcendentals=0),
        name="steps",
    )(fwd_state, adj_state, courant, decay_rate, strength, side, above, below, footprint, owner_map)


def shards(fwd_state, adj_state, courant, decay_rate, strength, footprint, owner_map):
    groups = lax.axis_size("emit")
    tiles = lax.axis_size("vx")
    rows = courant.shape[0]
    fields = [in_hbm(field) for field in (fwd_state, adj_state, courant, decay_rate, strength)]
    side, top, low = pack(*fields)
    side = lax.ppermute(side, "vy", [(0, 1), (1, 0)])
    corners = (HALO * FIELDS, 0)
    top = lax.dynamic_update_slice(top, side[:HALO], corners)
    low = lax.dynamic_update_slice(low, side[rows - HALO :], corners)
    below = lax.ppermute(top, "vx", [(i + 1, i) for i in range(tiles - 1)])
    above = lax.ppermute(low, "vx", [(i, i + 1) for i in range(tiles - 1)])
    ordered, pressure = run_steps(
        1.0 / groups, *fields, side, above, below, in_hbm(footprint.reshape(-1)), in_hbm(owner_map.reshape(-1))
    )
    sent = lax.all_to_all(ordered, "emit", 0, 0, tiled=True)
    gradient = jnp.sum(sent.reshape(groups, -1, BR, BC), axis=0)
    return gradient, pressure


def solution(mesh):
    in_specs = (
        P(None, "emit", "vx", "vy"),
        P(None, "emit", "vx", "vy"),
        P("vx", "vy"),
        P("vx", "vy"),
        P("vx", "vy"),
        P("emit", "vx", "vy", None),
        P("vx", "vy", None),
    )
    out_specs = (P("emit", "vx", "vy"), P("emit", "vx", "vy"))
    return jax.shard_map(shards, mesh=mesh, in_specs=in_specs, out_specs=out_specs, check_vma=False)
```

```python
import jax
import jax.numpy as jnp
from jax import lax
from jax.experimental import pallas as pl
from jax.experimental.pallas import tpu as pltpu
from jax.sharding import PartitionSpec as P

BR = 16
BC = 128
STEPS = 4
HALO = 4
SUB = 8
LANES = 128
FIELDS = 9
TILE_AT = 2 * SUB
VMEM_LIMIT = 40 * 1024 * 1024


def in_hbm(array):
    return pltpu.with_memory_space_constraint(array, pltpu.HBM)


def pack_kernel(fwd, adj, courant, decay, strength, side_out, top_out, low_out, cols, tops, lows, sem):
    rows = courant.shape[0]
    vy = lax.axis_index("vy")
    edge = pl.ds(pl.multiple_of((1 - vy) * LANES, LANES), LANES)
    copies = []
    for number, state in enumerate((fwd, adj)):
        at = pl.ds(3 * number, 3)
        copies.append((state.at[:, 0, :, edge], cols.at[at]))
        copies.append((state.at[:, 0, pl.ds(0, SUB), :], tops.at[at]))
        copies.append((state.at[:, 0, pl.ds(rows - SUB, SUB), :], lows.at[at]))
    for number, field in enumerate((courant, decay, strength)):
        copies.append((field.at[:, edge], cols.at[6 + number]))
        copies.append((field.at[pl.ds(0, SUB), :], tops.at[6 + number]))
        copies.append((field.at[pl.ds(rows - SUB, SUB), :], lows.at[6 + number]))
    started = [pltpu.make_async_copy(src, dst, sem.at[n]) for n, (src, dst) in enumerate(copies)]
    for copy in started:
        copy.start()
    for copy in started:
        copy.wait()
    lane = lax.broadcasted_iota(jnp.int32, (SUB, LANES), 1)

    for at in range(0, rows, SUB):
        packed = jnp.zeros((SUB, LANES), jnp.float32)
        for field in range(FIELDS):
            moved = pltpu.roll(cols[field, at : at + SUB, :], HALO * field + HALO * (1 - vy), 1)
            here = (lane >= HALO * field) & (lane < HALO * (field + 1))
            packed = jnp.where(here, moved, packed)
        side_out[at : at + SUB, :] = packed
    for out, edges, first in ((top_out, tops, 0), (low_out, lows, SUB - HALO)):
        for field in range(FIELDS):
            out[HALO * field : HALO * (field + 1), :] = edges[field, first : first + HALO, :]
        out[HALO * FIELDS : HALO * (FIELDS + 1), :] = jnp.zeros((HALO, 2 * LANES), jnp.float32)


def pack(fwd_state, adj_state, courant, decay_rate, strength):
    rows, columns = courant.shape
    edge = jax.ShapeDtypeStruct((HALO * (FIELDS + 1), columns), jnp.float32)
    return pl.pallas_call(
        pack_kernel,
        out_shape=(jax.ShapeDtypeStruct((rows, LANES), jnp.float32), edge, edge),
        in_specs=[pl.BlockSpec(memory_space=pltpu.HBM)] * 5,
        out_specs=[pl.BlockSpec(memory_space=pltpu.VMEM)] * 3,
        scratch_shapes=[
            pltpu.VMEM((FIELDS, rows, LANES), jnp.float32),
            pltpu.VMEM((FIELDS, SUB, columns), jnp.float32),
            pltpu.VMEM((FIELDS, SUB, columns), jnp.float32),
            pltpu.SemaphoreType.DMA((15,)),
        ],
        compiler_params=pltpu.CompilerParams(vmem_limit_bytes=VMEM_LIMIT),
        cost_estimate=pl.CostEstimate(flops=600000, bytes_accessed=1500000, transcendentals=0),
        name="pack",
    )(fwd_state, adj_state, courant, decay_rate, strength)


def half_kernel(
    lower_half, fwd, adj, courant, decay, strength, side,
    found_g, found_p, rim, held, coefs, starts, memories, fore, back, curves, partial, sem,
):
    whole = courant.shape[0]
    rows = whole // 2
    first_row = rows - SUB if lower_half else 0
    first_at = TILE_AT - SUB if lower_half else TILE_AT
    amount = rows + SUB
    vy = lax.axis_index("vy")
    copies = []
    for half in range(2):
        columns = pl.ds(half * LANES, LANES)
        source, target = pl.ds(first_row, amount), pl.ds(first_at, amount)
        for number, state in enumerate((fwd, adj)):
            copies.append((state.at[:, 0, source, columns], held.at[pl.ds(3 * number, 3), half, target, :]))
        for number, field in enumerate((courant, decay, strength)):
            copies.append((field.at[source, columns], held.at[6 + number, half, target, :]))
    started = [pltpu.make_async_copy(src, dst, sem.at[n]) for n, (src, dst) in enumerate(copies)]
    for copy in started:
        copy.start()

    lane = lax.broadcasted_iota(jnp.int32, (SUB, LANES), 1)
    beside = (lane >= (LANES - HALO) * vy) & (lane < (LANES - HALO) * vy + HALO)
    zero = jnp.zeros((SUB, LANES), jnp.float32)
    lane_first, lane_last = lane == 0, lane == LANES - 1
    empty = rows + TILE_AT if lower_half else SUB
    for field in range(FIELDS):
        shift = lax.rem(LANES - HALO * field + (LANES - HALO) * vy, LANES)
        for at in range(0, amount, SUB):
            strip = pltpu.roll(side[first_row + at : first_row + at + SUB, :], shift, 1)
            held[field, 2, first_at + at : first_at + at + SUB, :] = jnp.where(beside, strip, zero)
        for part in range(3):
            held[field, part, empty : empty + SUB, :] = zero
    for copy in started:
        copy.wait()
    rim_at = rows if lower_half else TILE_AT
    for field in range(FIELDS):
        for part in range(3):
            rim[field, part] = held[field, part, rim_at : rim_at + 2 * SUB, :]

    pitch = rows // SUB + 1

    def strips(field, part, t):
        return held[field, part, pl.ds(TILE_AT - HALO + t, SUB, stride=pitch), :]

    def advance(step, base_t, group):
        final = step == STEPS
        parts = range(2) if final else range(3)
        ts = [base_t + g for g in range(group)]
        stores = []
        speed, keep, loss = {}, {}, {}
        for part in parts:
            for g, t in enumerate(ts):
                for number, of in enumerate((speed, keep, loss)):
                    if step == 1:
                        of[part, g] = strips(6 + number, part, t)
                        stores.append((coefs, (number, part, SUB + t), of[part, g]))
                    else:
                        of[part, g] = coefs[number, part, SUB + t]
        results = []
        for own, state in ((fore, 0), (back, 1)):

            def level(number, part, t, own=own, state=state):
                if number >= 2:
                    return own[number - 2, part, SUB + t]
                if step == 1:
                    return strips(3 * state + number, part, t)
                return starts[state, part, SUB + t]

            centre = {
                (part, g): level(step, part, base_t + g)
                for part in range(3)
                for g in range(-1, group + 1)
                if part in parts or 0 <= g < group
            }
            seconds, nexts = {}, {}
            for g, t in enumerate(ts):
                right = [pltpu.roll(centre[part, g], LANES - 1, 1) for part in range(3)]
                left = [pltpu.roll(centre[part, g], 1, 1) for part in range(3)]
                for part in parts:
                    west = jnp.where(lane_first, left[(part + 2) % 3], left[part])
                    east = jnp.where(lane_last, right[(part + 1) % 3], right[part])
                    now = centre[part, g]
                    curve = (centre[part, g - 1] + centre[part, g + 1]) + (east + west) - 4.0 * now
                    memory = strips(3 * state + 2, part, t) if step == 1 else memories[state, part, SUB + t]
                    memory = keep[part, g] * memory + loss[part, g] * curve
                    second = speed[part, g] * (curve - memory)
                    following = 2.0 * now - level(step - 1, part, t) + second
                    if step == 1:
                        stores.append((starts, (state, part, SUB + t), now))
                    if not final:
                        stores.append((memories, (state, part, SUB + t), memory))
                        stores.append((own, (step - 1, part, SUB + t), following))
                    seconds[part, g] = second
                    nexts[part, g] = following
            results.append((seconds, nexts))
        (seconds, nexts), (_, adjoint) = results
        for part in range(2):
            for g, t in enumerate(ts):
                if step <= 2:
                    stores.append((curves, (step - 1, part, SUB + t), seconds[part, g]))
                    continue
                other = 4 - step
                value = (
                    seconds[part, g] * back[other, part, SUB + t] + curves[other, part, SUB + t] * adjoint[part, g]
                )
                if step == 3:
                    stores.append((partial, (part, SUB + t), value))
                else:
                    rows_at = pl.ds(HALO + t, SUB, stride=pitch)
                    stores.append((found_g, (part, rows_at), partial[part, SUB + t] + value))
                    stores.append((found_p, (part, rows_at), nexts[part, g]))
        for ref, index, value in stores:
            ref[index] = value

    for step in range(1, STEPS + 1):
        margin = STEPS - step
        count = pitch + 2 * margin
        advance(step, -margin, count)


def run_half(lower_half, fwd_state, adj_state, courant, decay_rate, strength, side):
    rows = courant.shape[0] // 2
    strip = (3, rows // SUB + 16, SUB, LANES)
    found = jax.ShapeDtypeStruct((2, rows + 4 * SUB, LANES), jnp.float32)
    return pl.pallas_call(
        lambda *refs: half_kernel(lower_half, *refs),
        out_shape=(found, found, jax.ShapeDtypeStruct((FIELDS, 3, 2 * SUB, LANES), jnp.float32)),
        in_specs=[pl.BlockSpec(memory_space=pltpu.HBM)] * 5 + [pl.BlockSpec(memory_space=pltpu.VMEM)],
        out_specs=[pl.BlockSpec(memory_space=pltpu.VMEM)] * 3,
        scratch_shapes=[
            pltpu.VMEM((FIELDS, 3, rows + 5 * SUB, LANES), jnp.float32),
            pltpu.VMEM((3,) + strip, jnp.float32),
            pltpu.VMEM((2,) + strip, jnp.float32),
            pltpu.VMEM((2,) + strip, jnp.float32),
            pltpu.VMEM((STEPS - 1,) + strip, jnp.float32),
            pltpu.VMEM((STEPS - 1,) + strip, jnp.float32),
            pltpu.VMEM((2,) + strip, jnp.float32),
            pltpu.VMEM(strip, jnp.float32),
            pltpu.SemaphoreType.DMA((10,)),
        ],
        compiler_params=pltpu.CompilerParams(vmem_limit_bytes=VMEM_LIMIT),
        cost_estimate=pl.CostEstimate(flops=8000000, bytes_accessed=1800000, transcendentals=0),
        name="lower_half" if lower_half else "upper_half",
    )(fwd_state, adj_state, courant, decay_rate, strength, side)


def rim_kernel(
    scale, upper_g, upper_p, upper_rim, lower_g, lower_p, lower_rim, above, below, footprint_in, owner_in,
    ordered, pressure, edges, footprint, owner, slot_of, gain_of, list_sem, out_sem,
):
    rows = pressure.shape[1]
    half_rows = rows // 2
    vy = lax.axis_index("vy")
    lists = [
        pltpu.make_async_copy(footprint_in, footprint, list_sem.at[0]),
        pltpu.make_async_copy(owner_in, owner, list_sem.at[1]),
    ]
    for copy in lists:
        copy.start()
    inner = half_rows - SUB
    leaving = []
    for half in range(2):
        columns = pl.ds(half * LANES, LANES)
        leaving.append((upper_p.at[half, pl.ds(2 * SUB, inner), :], pressure.at[0, pl.ds(SUB, inner), columns]))
        leaving.append((lower_p.at[half, pl.ds(SUB, inner), :], pressure.at[0, pl.ds(half_rows, inner), columns]))
    leaving = [pltpu.make_async_copy(src, dst, out_sem.at[n]) for n, (src, dst) in enumerate(leaving)]
    for copy in leaving:
        copy.start()

    lane = lax.broadcasted_iota(jnp.int32, (SUB, LANES), 1)
    sub = lax.broadcasted_iota(jnp.int32, (SUB, LANES), 0)
    beside = (lane >= (LANES - HALO) * vy) & (lane < (LANES - HALO) * vy + HALO)
    zero = jnp.zeros((SUB, LANES), jnp.float32)
    lane_first, lane_last = lane == 0, lane == LANES - 1
    first, last = sub == 0, sub == SUB - 1

    def halo_of(field, part, low):
        source = below if low else above
        last_pair = HALO * (FIELDS - 1)
        at = last_pair if part == 2 else (field // 2) * SUB
        value = source[at : at + SUB, (part % 2) * LANES : (part % 2 + 1) * LANES]
        in_lower_rows = part == 2 or field % 2 == 1
        if in_lower_rows == low:
            value = pltpu.roll(value, HALO, 0)
        value = jnp.where((sub < HALO) if low else (sub >= HALO), value, zero)
        if part == 2:
            shift = lax.rem(LANES - HALO * field + (LANES - HALO) * vy, LANES)
            value = jnp.where(beside, pltpu.roll(value, shift, 1), zero)
        return value

    def window(field, low):
        result = []
        for chunk in range(3):
            if low:
                row = [halo_of(field, p, True) if chunk == 2 else lower_rim[field, p, chunk * SUB : (chunk + 1) * SUB, :] for p in range(3)]
            else:
                row = [halo_of(field, p, False) if chunk == 0 else upper_rim[field, p, (chunk - 1) * SUB : chunk * SUB, :] for p in range(3)]
            result.append(row)
        return result

    for low in (False, True):
        speed, keep, loss = (window(field, low) for field in (6, 7, 8))
        states = [[window(3 * state + field, low) for field in range(3)] for state in range(2)]
        levels = ([], [])
        curves = []
        for step in range(1, STEPS + 1):
            chunks = (1,) if step == STEPS else (0, 1, 2)
            for state in range(2):
                old, new, memory = states[state]
                up = [[pltpu.roll(value, 1, 0) for value in row] for row in new]
                down = [[pltpu.roll(value, SUB - 1, 0) for value in row] for row in new]
                memories = [list(row) for row in memory]
                nexts = [list(row) for row in new]
                for chunk in chunks:
                    right = [pltpu.roll(value, LANES - 1, 1) for value in new[chunk]]
                    left = [pltpu.roll(value, 1, 1) for value in new[chunk]]
                    for part in range(2) if step == STEPS else range(3):
                        now = new[chunk][part]
                        north = jnp.where(first, up[chunk - 1][part] if chunk > 0 else zero, up[chunk][part])
                        south = jnp.where(last, down[chunk + 1][part] if chunk < 2 else zero, down[chunk][part])
                        west = jnp.where(lane_first, left[(part + 2) % 3], left[part])
                        east = jnp.where(lane_last, right[(part + 1) % 3], right[part])
                        curve = (north + south) + (east + west) - 4.0 * now
                        held = keep[chunk][part] * memory[chunk][part] + loss[chunk][part] * curve
                        second = speed[chunk][part] * (curve - held)
                        memories[chunk][part] = held
                        nexts[chunk][part] = 2.0 * now - old[chunk][part] + second
                        if state == 0 and chunk == 1 and part < 2:
                            curves.append(second)
                levels[state].append(nexts[1])
                states[state] = [new, nexts, memories]
        at = slice(SUB, 2 * SUB) if low else slice(0, SUB)
        for part in range(2):
            adjoint = [level[part] for level in levels[1]]
            seconds = curves[part::2]
            value = seconds[2] * adjoint[1] + seconds[1] * adjoint[2]
            value = value + (seconds[3] * adjoint[0] + seconds[0] * adjoint[3])
            edges[0, at, part * LANES : (part + 1) * LANES] = levels[0][STEPS - 1][part]
            edges[1, at, part * LANES : (part + 1) * LANES] = value
    outer = [
        pltpu.make_async_copy(edges.at[0, pl.ds(0, SUB), :], pressure.at[0, pl.ds(0, SUB), :], out_sem.at[4]),
        pltpu.make_async_copy(edges.at[0, pl.ds(SUB, SUB), :], pressure.at[0, pl.ds(rows - SUB, SUB), :], out_sem.at[5]),
    ]
    for copy in outer:
        copy.start()

    for copy in lists:
        copy.wait()
    blocks = gain_of.shape[0]
    for block in range(blocks):
        gain_of[block] = jnp.float32(0.0)
    for number in range(footprint.shape[0]):
        gain_of[footprint[number]] = jnp.float32(scale)
    for number in range(owner.shape[0]):
        slot_of[owner[number]] = number
    for block in range(blocks):
        source = upper_g if block < blocks // 2 else lower_g
        part = block % 2
        at = SUB + (block % (blocks // 2)) // 2 * BR
        slot, gain = slot_of[block], gain_of[block]
        high, low = source[part, at : at + SUB, :], source[part, at + SUB : at + BR, :]
        if block < 2:
            high = edges[1, 0:SUB, part * LANES : (part + 1) * LANES]
        if block >= blocks - 2:
            low = edges[1, SUB : 2 * SUB, part * LANES : (part + 1) * LANES]
        ordered[slot, 0:SUB, :] = high * gain
        ordered[slot, SUB:BR, :] = low * gain
    for copy in leaving + outer:
        copy.wait()


def run_rim(scale, upper, lower, above, below, footprint, owner_map):
    columns = above.shape[1]
    rows = 2 * (upper[0].shape[1] - 4 * SUB)
    blocks = owner_map.shape[0]
    return pl.pallas_call(
        lambda *refs: rim_kernel(scale, *refs),
        out_shape=(
            jax.ShapeDtypeStruct((blocks, BR, BC), jnp.float32),
            jax.ShapeDtypeStruct((1, rows, columns), jnp.float32),
        ),
        in_specs=[pl.BlockSpec(memory_space=pltpu.VMEM)] * 8 + [pl.BlockSpec(memory_space=pltpu.HBM)] * 2,
        out_specs=[pl.BlockSpec(memory_space=pltpu.VMEM), pl.BlockSpec(memory_space=pltpu.HBM)],
        scratch_shapes=[
            pltpu.VMEM((2, 2 * SUB, columns), jnp.float32),
            pltpu.SMEM(footprint.shape, jnp.int32),
            pltpu.SMEM((blocks,), jnp.int32),
            pltpu.SMEM((blocks,), jnp.int32),
            pltpu.SMEM((blocks,), jnp.float32),
            pltpu.SemaphoreType.DMA((2,)),
            pltpu.SemaphoreType.DMA((6,)),
        ],
        compiler_params=pltpu.CompilerParams(vmem_limit_bytes=VMEM_LIMIT),
        cost_estimate=pl.CostEstimate(flops=2000000, bytes_accessed=1500000, transcendentals=0),
        name="rim",
    )(*upper, *lower, above, below, footprint, owner_map)


def shards(fwd_state, adj_state, courant, decay_rate, strength, footprint, owner_map):
    groups = lax.axis_size("emit")
    tiles = lax.axis_size("vx")
    rows = courant.shape[0]
    fields = [in_hbm(field) for field in (fwd_state, adj_state, courant, decay_rate, strength)]
    side, top, low = pack(*fields)
    side = lax.ppermute(side, "vy", [(0, 1), (1, 0)])
    corners = (HALO * FIELDS, 0)
    top = lax.dynamic_update_slice(top, side[:HALO], corners)
    low = lax.dynamic_update_slice(low, side[rows - HALO :], corners)
    below = lax.ppermute(top, "vx", [(i + 1, i) for i in range(tiles - 1)])
    upper = run_half(False, *fields, side)
    low, upper = lax.optimization_barrier((low, upper))
    above = lax.ppermute(low, "vx", [(i, i + 1) for i in range(tiles - 1)])
    lower = run_half(True, *fields, side)
    ordered, pressure = run_rim(
        1.0 / groups, upper, lower, above, below, in_hbm(footprint.reshape(-1)), in_hbm(owner_map.reshape(-1))
    )
    sent = lax.all_to_all(ordered, "emit", 0, 0, tiled=True)
    gradient = jnp.sum(sent.reshape(groups, -1, BR, BC), axis=0)
    return gradient, pressure


def solution(mesh):
    in_specs = (
        P(None, "emit", "vx", "vy"),
        P(None, "emit", "vx", "vy"),
        P("vx", "vy"),
        P("vx", "vy"),
        P("vx", "vy"),
        P("emit", "vx", "vy", None),
        P("vx", "vy", None),
    )
    out_specs = (P("emit", "vx", "vy"), P("emit", "vx", "vy"))
    return jax.shard_map(shards, mesh=mesh, in_specs=in_specs, out_specs=out_specs, check_vma=False)
```

```python
import jax
import jax.numpy as jnp
from jax import lax
from jax.experimental import pallas as pl
from jax.experimental.pallas import tpu as pltpu
from jax.sharding import PartitionSpec as P

BR = 16
BC = 128
STEPS = 4
HALO = 4
SUB = 8
LANES = 128
FIELDS = 9
TILE_AT = 2 * SUB
VMEM_LIMIT = 28 * 1024 * 1024
GROUP = (13, 37, 35, 33)


def in_hbm(array):
    return pltpu.with_memory_space_constraint(array, pltpu.HBM)


def pack_kernel(fwd, adj, courant, decay, strength, side_out, top_out, low_out, cols, tops, lows, sem):
    rows = courant.shape[0]
    vy = lax.axis_index("vy")
    edge = pl.ds(pl.multiple_of((1 - vy) * LANES, LANES), LANES)
    copies = []
    for number, state in enumerate((fwd, adj)):
        at = pl.ds(3 * number, 3)
        copies.append((state.at[:, 0, :, edge], cols.at[at]))
        copies.append((state.at[:, 0, pl.ds(0, SUB), :], tops.at[at]))
        copies.append((state.at[:, 0, pl.ds(rows - SUB, SUB), :], lows.at[at]))
    for number, field in enumerate((courant, decay, strength)):
        copies.append((field.at[:, edge], cols.at[6 + number]))
        copies.append((field.at[pl.ds(0, SUB), :], tops.at[6 + number]))
        copies.append((field.at[pl.ds(rows - SUB, SUB), :], lows.at[6 + number]))
    started = [pltpu.make_async_copy(src, dst, sem.at[n]) for n, (src, dst) in enumerate(copies)]
    for copy in started:
        copy.start()
    lane = lax.broadcasted_iota(jnp.int32, (SUB, LANES), 1)
    packed = [jnp.zeros((SUB, LANES), jnp.float32)] * (rows // SUB)
    for number, members in enumerate(((0, 1, 2), (3, 4, 5), (6,), (7,), (8,))):
        started[3 * number].wait()
        for field in members:
            here = (lane >= HALO * field) & (lane < HALO * (field + 1))
            shift = HALO * field + HALO * (1 - vy)
            for at in range(rows // SUB):
                packed[at] = jnp.where(here, pltpu.roll(cols[field, at * SUB : (at + 1) * SUB, :], shift, 1), packed[at])
    for at in range(rows // SUB):
        side_out[at * SUB : (at + 1) * SUB, :] = packed[at]
    for number, copy in enumerate(started):
        if number % 3:
            copy.wait()
    for out, edges, first in ((top_out, tops, 0), (low_out, lows, SUB - HALO)):
        for field in range(FIELDS):
            out[HALO * field : HALO * (field + 1), :] = edges[field, first : first + HALO, :]
        out[HALO * FIELDS : HALO * (FIELDS + 1), :] = jnp.zeros((HALO, 2 * LANES), jnp.float32)


def pack(fwd_state, adj_state, courant, decay_rate, strength):
    rows, columns = courant.shape
    edge = jax.ShapeDtypeStruct((HALO * (FIELDS + 1), columns), jnp.float32)
    return pl.pallas_call(
        pack_kernel,
        out_shape=(jax.ShapeDtypeStruct((rows, LANES), jnp.float32), edge, edge),
        in_specs=[pl.BlockSpec(memory_space=pltpu.HBM)] * 5,
        out_specs=[pl.BlockSpec(memory_space=pltpu.VMEM)] * 3,
        scratch_shapes=[
            pltpu.VMEM((FIELDS, rows, LANES), jnp.float32),
            pltpu.VMEM((FIELDS, SUB, columns), jnp.float32),
            pltpu.VMEM((FIELDS, SUB, columns), jnp.float32),
            pltpu.SemaphoreType.DMA((15,)),
        ],
        compiler_params=pltpu.CompilerParams(vmem_limit_bytes=VMEM_LIMIT),
        cost_estimate=pl.CostEstimate(flops=600000, bytes_accessed=1500000, transcendentals=0),
        name="pack",
    )(fwd_state, adj_state, courant, decay_rate, strength)


def tile_kernel(
    fwd, adj, courant, decay, strength, side,
    found_g, found_p, rim, held, coefs, starts, memories, fore, back, curves, partial, sem,
):
    rows = courant.shape[0]
    vy = lax.axis_index("vy")
    copies = []
    for half in range(2):
        columns, target = pl.ds(half * LANES, LANES), pl.ds(TILE_AT, rows)
        for number, state in enumerate((fwd, adj)):
            copies.append((state.at[:, 0, :, columns], held.at[pl.ds(3 * number, 3), half, target, :]))
        for number, field in enumerate((courant, decay, strength)):
            copies.append((field.at[:, columns], held.at[6 + number, half, target, :]))
    started = [pltpu.make_async_copy(src, dst, sem.at[n]) for n, (src, dst) in enumerate(copies)]
    for copy in started:
        copy.start()

    lane = lax.broadcasted_iota(jnp.int32, (SUB, LANES), 1)
    beside = (lane >= (LANES - HALO) * vy) & (lane < (LANES - HALO) * vy + HALO)
    zero = jnp.zeros((SUB, LANES), jnp.float32)
    lane_first, lane_last = lane == 0, lane == LANES - 1
    for field in range(FIELDS):
        shift = lax.rem(LANES - HALO * field + (LANES - HALO) * vy, LANES)
        for at in range(0, rows, SUB):
            strip = pltpu.roll(side[at : at + SUB, :], shift, 1)
            held[field, 2, TILE_AT + at : TILE_AT + at + SUB, :] = jnp.where(beside, strip, zero)
        for part in range(3):
            held[field, part, SUB : 2 * SUB, :] = zero
            held[field, part, rows + 2 * SUB : rows + 3 * SUB, :] = zero
    for copy in started:
        copy.wait()
    for field in range(FIELDS):
        for part in range(3):
            rim[0, field, part] = held[field, part, TILE_AT : TILE_AT + 2 * SUB, :]
            rim[1, field, part] = held[field, part, rows : rows + 2 * SUB, :]

    pitch = rows // SUB + 1

    def strips(field, part, t):
        return held[field, part, pl.ds(TILE_AT - HALO + t, SUB, stride=pitch), :]

    def advance(step, base_t, group):
        final = step == STEPS
        parts = range(2) if final else range(3)
        ts = [base_t + g for g in range(group)]
        stores = []
        speed, keep, loss = {}, {}, {}
        for part in parts:
            for g, t in enumerate(ts):
                for number, of in enumerate((speed, keep, loss)):
                    if step == 1:
                        of[part, g] = strips(6 + number, part, t)
                        stores.append((coefs, (number, part, SUB + t), of[part, g]))
                    else:
                        of[part, g] = coefs[number, part, SUB + t]
        results = []
        for own, state in ((fore, 0), (back, 1)):

            def level(number, part, t, own=own, state=state):
                if number >= 2:
                    return own[number - 2, part, SUB + t]
                if step == 1:
                    return strips(3 * state + number, part, t)
                return starts[state, part, SUB + t]

            centre = {
                (part, g): level(step, part, base_t + g)
                for part in range(3)
                for g in range(-1, group + 1)
                if part in parts or 0 <= g < group
            }
            seconds, nexts = {}, {}
            for g, t in enumerate(ts):
                right = [pltpu.roll(centre[part, g], LANES - 1, 1) for part in range(3)]
                left = [pltpu.roll(centre[part, g], 1, 1) for part in range(3)]
                for part in parts:
                    west = jnp.where(lane_first, left[(part + 2) % 3], left[part])
                    east = jnp.where(lane_last, right[(part + 1) % 3], right[part])
                    now = centre[part, g]
                    curve = (centre[part, g - 1] + centre[part, g + 1]) + (east + west) - 4.0 * now
                    memory = strips(3 * state + 2, part, t) if step == 1 else memories[state, part, SUB + t]
                    memory = keep[part, g] * memory + loss[part, g] * curve
                    second = speed[part, g] * (curve - memory)
                    following = 2.0 * now - level(step - 1, part, t) + second
                    if step == 1:
                        stores.append((starts, (state, part, SUB + t), now))
                    if not final:
                        stores.append((memories, (state, part, SUB + t), memory))
                        stores.append((own, (step - 1, part, SUB + t), following))
                    seconds[part, g] = second
                    nexts[part, g] = following
            results.append((seconds, nexts))
        (seconds, nexts), (_, adjoint) = results
        for part in range(2):
            for g, t in enumerate(ts):
                if step <= 2:
                    stores.append((curves, (step - 1, part, SUB + t), seconds[part, g]))
                    continue
                other = 4 - step
                value = (
                    seconds[part, g] * back[other, part, SUB + t] + curves[other, part, SUB + t] * adjoint[part, g]
                )
                if step == 3:
                    stores.append((partial, (part, SUB + t), value))
                else:
                    rows_at = pl.ds(HALO + t, SUB, stride=pitch)
                    stores.append((found_g, (part, rows_at), partial[part, SUB + t] + value))
                    stores.append((found_p, (part, rows_at), nexts[part, g]))
        for ref, index, value in stores:
            ref[index] = value

    for step in range(1, STEPS + 1):
        margin = STEPS - step
        count = pitch + 2 * margin
        group = GROUP[step - 1]
        if count == group:
            advance(step, -margin, group)
        else:

            def turn(number, carry, step=step, margin=margin, group=group):
                advance(step, number * group - margin, group)
                return carry

            lax.fori_loop(0, count // group, turn, 0)


def run_tile(fwd_state, adj_state, courant, decay_rate, strength, side):
    rows = courant.shape[0]
    strip = (3, rows // SUB + 16, SUB, LANES)
    found = jax.ShapeDtypeStruct((2, rows + 6 * SUB, LANES), jnp.float32)
    return pl.pallas_call(
        tile_kernel,
        out_shape=(found, found, jax.ShapeDtypeStruct((2, FIELDS, 3, 2 * SUB, LANES), jnp.float32)),
        in_specs=[pl.BlockSpec(memory_space=pl.ANY)] * 5 + [pl.BlockSpec(memory_space=pltpu.VMEM)],
        out_specs=[pl.BlockSpec(memory_space=pltpu.VMEM)] * 3,
        scratch_shapes=[
            pltpu.VMEM((FIELDS, 3, rows + 7 * SUB, LANES), jnp.float32),
            pltpu.VMEM((3,) + strip, jnp.float32),
            pltpu.VMEM((2,) + strip, jnp.float32),
            pltpu.VMEM((2,) + strip, jnp.float32),
            pltpu.VMEM((STEPS - 1,) + strip, jnp.float32),
            pltpu.VMEM((STEPS - 1,) + strip, jnp.float32),
            pltpu.VMEM((2,) + strip, jnp.float32),
            pltpu.VMEM(strip, jnp.float32),
            pltpu.SemaphoreType.DMA((10,)),
        ],
        compiler_params=pltpu.CompilerParams(vmem_limit_bytes=VMEM_LIMIT),
        cost_estimate=pl.CostEstimate(flops=14000000, bytes_accessed=3500000, transcendentals=0),
        name="tile",
    )(fwd_state, adj_state, courant, decay_rate, strength, side)


def rim_kernel(
    scale, found_g, found_p, rim, above, below, footprint_in, owner_in,
    ordered, pressure, edges, footprint, owner, slot_of, gain_of, list_sem, out_sem,
):
    rows = pressure.shape[1]
    vy = lax.axis_index("vy")
    lists = [
        pltpu.make_async_copy(footprint_in, footprint, list_sem.at[0]),
        pltpu.make_async_copy(owner_in, owner, list_sem.at[1]),
    ]
    for copy in lists:
        copy.start()
    inner = rows - 2 * SUB
    leaving = []
    for half in range(2):
        columns = pl.ds(half * LANES, LANES)
        leaving.append((found_p.at[half, pl.ds(2 * SUB, inner), :], pressure.at[0, pl.ds(SUB, inner), columns]))
    leaving = [pltpu.make_async_copy(src, dst, out_sem.at[n]) for n, (src, dst) in enumerate(leaving)]
    for copy in leaving:
        copy.start()

    lane = lax.broadcasted_iota(jnp.int32, (SUB, LANES), 1)
    sub = lax.broadcasted_iota(jnp.int32, (SUB, LANES), 0)
    beside = (lane >= (LANES - HALO) * vy) & (lane < (LANES - HALO) * vy + HALO)
    zero = jnp.zeros((SUB, LANES), jnp.float32)
    lane_first, lane_last = lane == 0, lane == LANES - 1
    first, last = sub == 0, sub == SUB - 1

    def halo_of(field, part, low):
        source = below if low else above
        last_pair = HALO * (FIELDS - 1)
        at = last_pair if part == 2 else (field // 2) * SUB
        value = source[at : at + SUB, (part % 2) * LANES : (part % 2 + 1) * LANES]
        in_lower_rows = part == 2 or field % 2 == 1
        if in_lower_rows == low:
            value = pltpu.roll(value, HALO, 0)
        value = jnp.where((sub < HALO) if low else (sub >= HALO), value, zero)
        if part == 2:
            shift = lax.rem(LANES - HALO * field + (LANES - HALO) * vy, LANES)
            value = jnp.where(beside, pltpu.roll(value, shift, 1), zero)
        return value

    def window(field, low):
        result = []
        for chunk in range(3):
            if low:
                row = [halo_of(field, p, True) if chunk == 2 else rim[1, field, p, chunk * SUB : (chunk + 1) * SUB, :] for p in range(3)]
            else:
                row = [halo_of(field, p, False) if chunk == 0 else rim[0, field, p, (chunk - 1) * SUB : chunk * SUB, :] for p in range(3)]
            result.append(row)
        return result

    for low in (False, True):
        speed, keep, loss = (window(field, low) for field in (6, 7, 8))
        states = [[window(3 * state + field, low) for field in range(3)] for state in range(2)]
        levels = ([], [])
        curves = []
        for step in range(1, STEPS + 1):
            chunks = (1,) if step == STEPS else (0, 1, 2)
            for state in range(2):
                old, new, memory = states[state]
                up = [[pltpu.roll(value, 1, 0) for value in row] for row in new]
                down = [[pltpu.roll(value, SUB - 1, 0) for value in row] for row in new]
                memories = [list(row) for row in memory]
                nexts = [list(row) for row in new]
                for chunk in chunks:
                    right = [pltpu.roll(value, LANES - 1, 1) for value in new[chunk]]
                    left = [pltpu.roll(value, 1, 1) for value in new[chunk]]
                    for part in range(2) if step == STEPS else range(3):
                        now = new[chunk][part]
                        north = jnp.where(first, up[chunk - 1][part] if chunk > 0 else zero, up[chunk][part])
                        south = jnp.where(last, down[chunk + 1][part] if chunk < 2 else zero, down[chunk][part])
                        west = jnp.where(lane_first, left[(part + 2) % 3], left[part])
                        east = jnp.where(lane_last, right[(part + 1) % 3], right[part])
                        curve = (north + south) + (east + west) - 4.0 * now
                        held = keep[chunk][part] * memory[chunk][part] + loss[chunk][part] * curve
                        second = speed[chunk][part] * (curve - held)
                        memories[chunk][part] = held
                        nexts[chunk][part] = 2.0 * now - old[chunk][part] + second
                        if state == 0 and chunk == 1 and part < 2:
                            curves.append(second)
                levels[state].append(nexts[1])
                states[state] = [new, nexts, memories]
        at = slice(SUB, 2 * SUB) if low else slice(0, SUB)
        for part in range(2):
            adjoint = [level[part] for level in levels[1]]
            seconds = curves[part::2]
            value = seconds[2] * adjoint[1] + seconds[1] * adjoint[2]
            value = value + (seconds[3] * adjoint[0] + seconds[0] * adjoint[3])
            edges[0, at, part * LANES : (part + 1) * LANES] = levels[0][STEPS - 1][part]
            edges[1, at, part * LANES : (part + 1) * LANES] = value
    outer = [
        pltpu.make_async_copy(edges.at[0, pl.ds(0, SUB), :], pressure.at[0, pl.ds(0, SUB), :], out_sem.at[2]),
        pltpu.make_async_copy(edges.at[0, pl.ds(SUB, SUB), :], pressure.at[0, pl.ds(rows - SUB, SUB), :], out_sem.at[3]),
    ]
    for copy in outer:
        copy.start()

    for copy in lists:
        copy.wait()
    blocks = gain_of.shape[0]
    for block in range(blocks):
        gain_of[block] = jnp.float32(0.0)
    for number in range(footprint.shape[0]):
        gain_of[footprint[number]] = jnp.float32(scale)
    for number in range(owner.shape[0]):
        slot_of[owner[number]] = number
    for block in range(blocks):
        part = block % 2
        at = SUB + block // 2 * BR
        slot, gain = slot_of[block], gain_of[block]
        high, low = found_g[part, at : at + SUB, :], found_g[part, at + SUB : at + BR, :]
        if block < 2:
            high = edges[1, 0:SUB, part * LANES : (part + 1) * LANES]
        if block >= blocks - 2:
            low = edges[1, SUB : 2 * SUB, part * LANES : (part + 1) * LANES]
        ordered[slot, 0:SUB, :] = high * gain
        ordered[slot, SUB:BR, :] = low * gain
    for copy in leaving + outer:
        copy.wait()


def run_rim(scale, found, above, below, footprint, owner_map):
    columns = above.shape[1]
    rows = found[0].shape[1] - 6 * SUB
    blocks = owner_map.shape[0]
    return pl.pallas_call(
        lambda *refs: rim_kernel(scale, *refs),
        out_shape=(
            jax.ShapeDtypeStruct((blocks, BR, BC), jnp.float32),
            jax.ShapeDtypeStruct((1, rows, columns), jnp.float32),
        ),
        in_specs=[pl.BlockSpec(memory_space=pltpu.VMEM)] * 5 + [pl.BlockSpec(memory_space=pltpu.HBM)] * 2,
        out_specs=[pl.BlockSpec(memory_space=pltpu.VMEM), pl.BlockSpec(memory_space=pltpu.HBM)],
        scratch_shapes=[
            pltpu.VMEM((2, 2 * SUB, columns), jnp.float32),
            pltpu.SMEM(footprint.shape, jnp.int32),
            pltpu.SMEM((blocks,), jnp.int32),
            pltpu.SMEM((blocks,), jnp.int32),
            pltpu.SMEM((blocks,), jnp.float32),
            pltpu.SemaphoreType.DMA((2,)),
            pltpu.SemaphoreType.DMA((4,)),
        ],
        compiler_params=pltpu.CompilerParams(vmem_limit_bytes=VMEM_LIMIT),
        cost_estimate=pl.CostEstimate(flops=2000000, bytes_accessed=1500000, transcendentals=0),
        name="rim",
    )(*found, above, below, footprint, owner_map)


def shards(fwd_state, adj_state, courant, decay_rate, strength, footprint, owner_map):
    groups = lax.axis_size("emit")
    tiles = lax.axis_size("vx")
    rows = courant.shape[0]
    fields = (fwd_state, adj_state, courant, decay_rate, strength)
    side, top, low = pack(*[in_hbm(field) for field in fields])
    later, side = lax.optimization_barrier((fields, side))
    side = lax.ppermute(side, "vy", [(0, 1), (1, 0)])
    corners = (HALO * FIELDS, 0)
    top = lax.dynamic_update_slice(top, side[:HALO], corners)
    low = lax.dynamic_update_slice(low, side[rows - HALO :], corners)
    below = lax.ppermute(top, "vx", [(i + 1, i) for i in range(tiles - 1)])
    above = lax.ppermute(low, "vx", [(i, i + 1) for i in range(tiles - 1)])
    found = run_tile(*later, side)
    ordered, pressure = run_rim(
        1.0 / groups, found, above, below, in_hbm(footprint.reshape(-1)), in_hbm(owner_map.reshape(-1))
    )
    sent = lax.all_to_all(ordered, "emit", 0, 0, tiled=True)
    gradient = jnp.sum(sent.reshape(groups, -1, BR, BC), axis=0)
    return gradient, pressure


def solution(mesh):
    in_specs = (
        P(None, "emit", "vx", "vy"),
        P(None, "emit", "vx", "vy"),
        P("vx", "vy"),
        P("vx", "vy"),
        P("vx", "vy"),
        P("emit", "vx", "vy", None),
        P("vx", "vy", None),
    )
    out_specs = (P("emit", "vx", "vy"), P("emit", "vx", "vy"))
    return jax.shard_map(shards, mesh=mesh, in_specs=in_specs, out_specs=out_specs, check_vma=False)
```

```python
import jax
import jax.numpy as jnp
from jax import lax
from jax.experimental import pallas as pl
from jax.experimental.pallas import tpu as pltpu
from jax.sharding import PartitionSpec as P

BR = 16
BC = 128
STEPS = 4
HALO = 4
SUB = 8
LANES = 128
FIELDS = 9
TILE_AT = 2 * SUB
VMEM_LIMIT = 28 * 1024 * 1024
GROUP = (13, 37, 35, 33)


def in_hbm(array):
    return pltpu.with_memory_space_constraint(array, pltpu.HBM)


def pack_kernel(fwd, adj, courant, decay, strength, side_out, top_out, low_out, cols, tops, lows, sem):
    rows = courant.shape[0]
    vy = lax.axis_index("vy")
    edge = pl.ds(pl.multiple_of((1 - vy) * LANES, LANES), LANES)
    copies = []
    for number, state in enumerate((fwd, adj)):
        at = pl.ds(3 * number, 3)
        copies.append((state.at[:, 0, :, edge], cols.at[at]))
        copies.append((state.at[:, 0, pl.ds(0, SUB), :], tops.at[at]))
        copies.append((state.at[:, 0, pl.ds(rows - SUB, SUB), :], lows.at[at]))
    for number, field in enumerate((courant, decay, strength)):
        copies.append((field.at[:, edge], cols.at[6 + number]))
        copies.append((field.at[pl.ds(0, SUB), :], tops.at[6 + number]))
        copies.append((field.at[pl.ds(rows - SUB, SUB), :], lows.at[6 + number]))
    started = [pltpu.make_async_copy(src, dst, sem.at[n]) for n, (src, dst) in enumerate(copies)]
    for copy in started:
        copy.start()
    lane = lax.broadcasted_iota(jnp.int32, (SUB, LANES), 1)
    packed = [jnp.zeros((SUB, LANES), jnp.float32)] * (rows // SUB)
    for number, members in enumerate(((0, 1, 2), (3, 4, 5), (6,), (7,), (8,))):
        started[3 * number].wait()
        for field in members:
            here = (lane >= HALO * field) & (lane < HALO * (field + 1))
            shift = HALO * field + HALO * (1 - vy)
            for at in range(rows // SUB):
                packed[at] = jnp.where(here, pltpu.roll(cols[field, at * SUB : (at + 1) * SUB, :], shift, 1), packed[at])
    for at in range(rows // SUB):
        side_out[at * SUB : (at + 1) * SUB, :] = packed[at]
    for number, copy in enumerate(started):
        if number % 3:
            copy.wait()
    for out, edges, first in ((top_out, tops, 0), (low_out, lows, SUB - HALO)):
        for field in range(FIELDS):
            out[HALO * field : HALO * (field + 1), :] = edges[field, first : first + HALO, :]
        out[HALO * FIELDS : HALO * (FIELDS + 1), :] = jnp.zeros((HALO, 2 * LANES), jnp.float32)


def pack(fwd_state, adj_state, courant, decay_rate, strength):
    rows, columns = courant.shape
    edge = jax.ShapeDtypeStruct((HALO * (FIELDS + 1), columns), jnp.float32)
    return pl.pallas_call(
        pack_kernel,
        out_shape=(jax.ShapeDtypeStruct((rows, LANES), jnp.float32), edge, edge),
        in_specs=[pl.BlockSpec(memory_space=pltpu.HBM)] * 5,
        out_specs=[pl.BlockSpec(memory_space=pltpu.VMEM)] * 3,
        scratch_shapes=[
            pltpu.VMEM((FIELDS, rows, LANES), jnp.float32),
            pltpu.VMEM((FIELDS, SUB, columns), jnp.float32),
            pltpu.VMEM((FIELDS, SUB, columns), jnp.float32),
            pltpu.SemaphoreType.DMA((15,)),
        ],
        compiler_params=pltpu.CompilerParams(vmem_limit_bytes=VMEM_LIMIT),
        cost_estimate=pl.CostEstimate(flops=600000, bytes_accessed=1500000, transcendentals=0),
        name="pack",
    )(fwd_state, adj_state, courant, decay_rate, strength)


def tile_kernel(
    scale, fwd, adj, courant, decay, strength, side, footprint_in, owner_in,
    ordered, found_p, rim, marks, gains, held, coefs, starts, memories, fore, back, curves, partial, found_g,
    footprint, owner, slot_of, gain_of, list_sem,
):
    rows = courant.shape[0]
    lists = [
        pltpu.make_async_copy(footprint_in, footprint, list_sem.at[0]),
        pltpu.make_async_copy(owner_in, owner, list_sem.at[1]),
    ]
    for copy in lists:
        copy.start()
    vy = lax.axis_index("vy")
    lane = lax.broadcasted_iota(jnp.int32, (SUB, LANES), 1)
    beside = (lane >= (LANES - HALO) * vy) & (lane < (LANES - HALO) * vy + HALO)
    zero = jnp.zeros((SUB, LANES), jnp.float32)
    lane_first, lane_last = lane == 0, lane == LANES - 1
    for field in range(FIELDS):
        shift = lax.rem(LANES - HALO * field + (LANES - HALO) * vy, LANES)
        for at in range(0, rows, SUB):
            strip = pltpu.roll(side[at : at + SUB, :], shift, 1)
            held[field, 2, TILE_AT + at : TILE_AT + at + SUB, :] = jnp.where(beside, strip, zero)
        for part in range(3):
            held[field, part, SUB : 2 * SUB, :] = zero
            held[field, part, rows + 2 * SUB : rows + 3 * SUB, :] = zero
    for half in range(2):
        columns, target = slice(half * LANES, (half + 1) * LANES), slice(TILE_AT, TILE_AT + rows)
        for number in range(3):
            held[number, half, target, :] = fwd[number, 0, :, columns]
            held[3 + number, half, target, :] = adj[number, 0, :, columns]
        for number, field in enumerate((courant, decay, strength)):
            held[6 + number, half, target, :] = field[:, columns]
    for field in range(FIELDS):
        for part in range(3):
            rim[0, field, part] = held[field, part, TILE_AT : TILE_AT + 2 * SUB, :]
            rim[1, field, part] = held[field, part, rows : rows + 2 * SUB, :]

    pitch = rows // SUB + 1

    def strips(field, part, t):
        return held[field, part, pl.ds(TILE_AT - HALO + t, SUB, stride=pitch), :]

    def advance(step, base_t, group):
        final = step == STEPS
        parts = range(2) if final else range(3)
        ts = [base_t + g for g in range(group)]
        stores = []
        speed, keep, loss = {}, {}, {}
        for part in parts:
            for g, t in enumerate(ts):
                for number, of in enumerate((speed, keep, loss)):
                    if step == 1:
                        of[part, g] = strips(6 + number, part, t)
                        stores.append((coefs, (number, part, SUB + t), of[part, g]))
                    else:
                        of[part, g] = coefs[number, part, SUB + t]
        results = []
        for own, state in ((fore, 0), (back, 1)):

            def level(number, part, t, own=own, state=state):
                if number >= 2:
                    return own[number - 2, part, SUB + t]
                if step == 1:
                    return strips(3 * state + number, part, t)
                return starts[state, part, SUB + t]

            centre = {
                (part, g): level(step, part, base_t + g)
                for part in range(3)
                for g in range(-1, group + 1)
                if part in parts or 0 <= g < group
            }
            seconds, nexts = {}, {}
            for g, t in enumerate(ts):
                right = [pltpu.roll(centre[part, g], LANES - 1, 1) for part in range(3)]
                left = [pltpu.roll(centre[part, g], 1, 1) for part in range(3)]
                for part in parts:
                    west = jnp.where(lane_first, left[(part + 2) % 3], left[part])
                    east = jnp.where(lane_last, right[(part + 1) % 3], right[part])
                    now = centre[part, g]
                    curve = (centre[part, g - 1] + centre[part, g + 1]) + (east + west) - 4.0 * now
                    memory = strips(3 * state + 2, part, t) if step == 1 else memories[state, part, SUB + t]
                    memory = keep[part, g] * memory + loss[part, g] * curve
                    second = speed[part, g] * (curve - memory)
                    following = 2.0 * now - level(step - 1, part, t) + second
                    if step == 1:
                        stores.append((starts, (state, part, SUB + t), now))
                    if not final:
                        stores.append((memories, (state, part, SUB + t), memory))
                        stores.append((own, (step - 1, part, SUB + t), following))
                    seconds[part, g] = second
                    nexts[part, g] = following
            results.append((seconds, nexts))
        (seconds, nexts), (_, adjoint) = results
        for part in range(2):
            for g, t in enumerate(ts):
                if step <= 2:
                    stores.append((curves, (step - 1, part, SUB + t), seconds[part, g]))
                    continue
                other = 4 - step
                value = (
                    seconds[part, g] * back[other, part, SUB + t] + curves[other, part, SUB + t] * adjoint[part, g]
                )
                if step == 3:
                    stores.append((partial, (part, SUB + t), value))
                else:
                    rows_at = pl.ds(HALO + t, SUB, stride=pitch)
                    stores.append((found_g, (part, rows_at), partial[part, SUB + t] + value))
                    stores.append((found_p, (part, rows_at), nexts[part, g]))
        for ref, index, value in stores:
            ref[index] = value

    for step in range(1, STEPS + 1):
        margin = STEPS - step
        count = pitch + 2 * margin
        group = GROUP[step - 1]
        if count == group:
            advance(step, -margin, group)
        else:

            def turn(number, carry, step=step, margin=margin, group=group):
                advance(step, number * group - margin, group)
                return carry

            lax.fori_loop(0, count // group, turn, 0)

    for copy in lists:
        copy.wait()
    blocks = gain_of.shape[0]
    for block in range(blocks):
        gain_of[block] = jnp.float32(0.0)
    for number in range(footprint.shape[0]):
        gain_of[footprint[number]] = jnp.float32(scale)
    for number in range(blocks):
        slot_of[owner[number]] = number
        marks[number] = jnp.full((SUB, LANES), owner[number], jnp.int32)
    for number, block in enumerate((0, 1, blocks - 2, blocks - 1)):
        gains[number] = jnp.full((SUB, LANES), gain_of[block], jnp.float32)
    for block in range(blocks):
        at = SUB + block // 2 * BR
        ordered[slot_of[block]] = found_g[block % 2, at : at + BR, :] * gain_of[block]


def run_tile(scale, fwd_state, adj_state, courant, decay_rate, strength, side, footprint, owner_map):
    rows = courant.shape[0]
    strip = (3, rows // SUB + 16, SUB, LANES)
    found = (2, rows + 6 * SUB, LANES)
    blocks = owner_map.shape[0]
    return pl.pallas_call(
        lambda *refs: tile_kernel(scale, *refs),
        out_shape=(
            jax.ShapeDtypeStruct((blocks, BR, BC), jnp.float32),
            jax.ShapeDtypeStruct(found, jnp.float32),
            jax.ShapeDtypeStruct((2, FIELDS, 3, 2 * SUB, LANES), jnp.float32),
            jax.ShapeDtypeStruct((blocks, SUB, LANES), jnp.int32),
            jax.ShapeDtypeStruct((4, SUB, LANES), jnp.float32),
        ),
        in_specs=[pl.BlockSpec(memory_space=pltpu.VMEM)] * 6 + [pl.BlockSpec(memory_space=pltpu.HBM)] * 2,
        out_specs=[pl.BlockSpec(memory_space=pltpu.VMEM)] * 5,
        scratch_shapes=[
            pltpu.VMEM((FIELDS, 3, rows + 7 * SUB, LANES), jnp.float32),
            pltpu.VMEM((3,) + strip, jnp.float32),
            pltpu.VMEM((2,) + strip, jnp.float32),
            pltpu.VMEM((2,) + strip, jnp.float32),
            pltpu.VMEM((STEPS - 1,) + strip, jnp.float32),
            pltpu.VMEM((STEPS - 1,) + strip, jnp.float32),
            pltpu.VMEM((2,) + strip, jnp.float32),
            pltpu.VMEM(strip, jnp.float32),
            pltpu.VMEM(found, jnp.float32),
            pltpu.SMEM(footprint.shape, jnp.int32),
            pltpu.SMEM((blocks,), jnp.int32),
            pltpu.SMEM((blocks,), jnp.int32),
            pltpu.SMEM((blocks,), jnp.float32),
            pltpu.SemaphoreType.DMA((2,)),
        ],
        compiler_params=pltpu.CompilerParams(vmem_limit_bytes=VMEM_LIMIT),
        cost_estimate=pl.CostEstimate(flops=14000000, bytes_accessed=3500000, transcendentals=0),
        name="tile",
    )(fwd_state, adj_state, courant, decay_rate, strength, side, footprint, owner_map)


def rim_kernel(slots, marks, gains, rim, above, below, ordered, edge_p):
    vy = lax.axis_index("vy")
    lane = lax.broadcasted_iota(jnp.int32, (SUB, LANES), 1)
    sub = lax.broadcasted_iota(jnp.int32, (SUB, LANES), 0)
    beside = (lane >= (LANES - HALO) * vy) & (lane < (LANES - HALO) * vy + HALO)
    zero = jnp.zeros((SUB, LANES), jnp.float32)
    lane_first, lane_last = lane == 0, lane == LANES - 1
    first, last = sub == 0, sub == SUB - 1

    def halo_of(field, part, low):
        source = below if low else above
        last_pair = HALO * (FIELDS - 1)
        at = last_pair if part == 2 else (field // 2) * SUB
        value = source[at : at + SUB, (part % 2) * LANES : (part % 2 + 1) * LANES]
        in_lower_rows = part == 2 or field % 2 == 1
        if in_lower_rows == low:
            value = pltpu.roll(value, HALO, 0)
        value = jnp.where((sub < HALO) if low else (sub >= HALO), value, zero)
        if part == 2:
            shift = lax.rem(LANES - HALO * field + (LANES - HALO) * vy, LANES)
            value = jnp.where(beside, pltpu.roll(value, shift, 1), zero)
        return value

    def window(field, low):
        result = []
        for chunk in range(3):
            if low:
                row = [halo_of(field, p, True) if chunk == 2 else rim[1, field, p, chunk * SUB : (chunk + 1) * SUB, :] for p in range(3)]
            else:
                row = [halo_of(field, p, False) if chunk == 0 else rim[0, field, p, (chunk - 1) * SUB : chunk * SUB, :] for p in range(3)]
            result.append(row)
        return result

    edges = {}
    for low in (False, True):
        speed, keep, loss = (window(field, low) for field in (6, 7, 8))
        states = [[window(3 * state + field, low) for field in range(3)] for state in range(2)]
        levels = ([], [])
        curves = []
        for step in range(1, STEPS + 1):
            chunks = (1,) if step == STEPS else (0, 1, 2)
            for state in range(2):
                old, new, memory = states[state]
                up = [[pltpu.roll(value, 1, 0) for value in row] for row in new]
                down = [[pltpu.roll(value, SUB - 1, 0) for value in row] for row in new]
                memories = [list(row) for row in memory]
                nexts = [list(row) for row in new]
                for chunk in chunks:
                    right = [pltpu.roll(value, LANES - 1, 1) for value in new[chunk]]
                    left = [pltpu.roll(value, 1, 1) for value in new[chunk]]
                    for part in range(2) if step == STEPS else range(3):
                        now = new[chunk][part]
                        north = jnp.where(first, up[chunk - 1][part] if chunk > 0 else zero, up[chunk][part])
                        south = jnp.where(last, down[chunk + 1][part] if chunk < 2 else zero, down[chunk][part])
                        west = jnp.where(lane_first, left[(part + 2) % 3], left[part])
                        east = jnp.where(lane_last, right[(part + 1) % 3], right[part])
                        curve = (north + south) + (east + west) - 4.0 * now
                        held = keep[chunk][part] * memory[chunk][part] + loss[chunk][part] * curve
                        second = speed[chunk][part] * (curve - held)
                        memories[chunk][part] = held
                        nexts[chunk][part] = 2.0 * now - old[chunk][part] + second
                        if state == 0 and chunk == 1 and part < 2:
                            curves.append(second)
                levels[state].append(nexts[1])
                states[state] = [new, nexts, memories]
        at = slice(SUB, 2 * SUB) if low else slice(0, SUB)
        for part in range(2):
            adjoint = [level[part] for level in levels[1]]
            seconds = curves[part::2]
            value = seconds[2] * adjoint[1] + seconds[1] * adjoint[2]
            value = value + (seconds[3] * adjoint[0] + seconds[0] * adjoint[3])
            edge_p[at, part * LANES : (part + 1) * LANES] = levels[0][STEPS - 1][part]
            edges[low, part] = value * gains[2 * low + part]

    blocks = slots.shape[0]
    for slot in range(blocks):
        block = marks[slot]
        high, low = slots[slot, 0:SUB, :], slots[slot, SUB:BR, :]
        for part in range(2):
            high = jnp.where(block == part, edges[False, part], high)
            low = jnp.where(block == blocks - 2 + part, edges[True, part], low)
        ordered[slot, 0:SUB, :] = high
        ordered[slot, SUB:BR, :] = low


def run_rim(slots, marks, gains, rim, above, below):
    return pl.pallas_call(
        rim_kernel,
        out_shape=(
            jax.ShapeDtypeStruct(slots.shape, jnp.float32),
            jax.ShapeDtypeStruct((2 * SUB, above.shape[1]), jnp.float32),
        ),
        in_specs=[pl.BlockSpec(memory_space=pltpu.VMEM)] * 6,
        out_specs=[pl.BlockSpec(memory_space=pltpu.VMEM)] * 2,
        compiler_params=pltpu.CompilerParams(vmem_limit_bytes=VMEM_LIMIT),
        cost_estimate=pl.CostEstimate(flops=2000000, bytes_accessed=1000000, transcendentals=0),
        name="rim",
    )(slots, marks, gains, rim, above, below)


def finish_kernel(sent, found_p, edge_p, gradient, pressure, total, sem):
    rows = pressure.shape[1]
    inner = rows - 2 * SUB
    copies = [
        (edge_p.at[pl.ds(0, SUB), :], pressure.at[0, pl.ds(0, SUB), :]),
        (edge_p.at[pl.ds(SUB, SUB), :], pressure.at[0, pl.ds(rows - SUB, SUB), :]),
    ]
    for half in range(2):
        columns = pl.ds(half * LANES, LANES)
        copies.append((found_p.at[half, pl.ds(2 * SUB, inner), :], pressure.at[0, pl.ds(SUB, inner), columns]))
    copies = [pltpu.make_async_copy(src, dst, sem.at[n]) for n, (src, dst) in enumerate(copies)]
    for copy in copies:
        copy.start()
    held = gradient.shape[0]
    for slot in range(held):
        terms = [sent[number] for number in range(slot, sent.shape[0], held)]
        while len(terms) > 1:
            joined = [one + two for one, two in zip(terms[::2], terms[1::2])]
            terms = joined + terms[2 * len(joined) :]
        total[slot] = terms[0]
    last = pltpu.make_async_copy(total, gradient, sem.at[4])
    last.start()
    last.wait()
    for copy in copies:
        copy.wait()


def finish(groups, sent, found_p, edge_p):
    gradient = (sent.shape[0] // groups, BR, BC)
    rows, columns = found_p.shape[1] - 6 * SUB, edge_p.shape[1]
    return pl.pallas_call(
        finish_kernel,
        out_shape=(
            jax.ShapeDtypeStruct(gradient, jnp.float32),
            jax.ShapeDtypeStruct((1, rows, columns), jnp.float32),
        ),
        in_specs=[pl.BlockSpec(memory_space=pltpu.VMEM)] * 3,
        out_specs=[pl.BlockSpec(memory_space=pltpu.HBM)] * 2,
        scratch_shapes=[pltpu.VMEM(gradient, jnp.float32), pltpu.SemaphoreType.DMA((5,))],
        compiler_params=pltpu.CompilerParams(vmem_limit_bytes=VMEM_LIMIT),
        cost_estimate=pl.CostEstimate(flops=70000, bytes_accessed=800000, transcendentals=0),
        name="finish",
    )(sent, found_p, edge_p)


def shards(fwd_state, adj_state, courant, decay_rate, strength, footprint, owner_map):
    groups = lax.axis_size("emit")
    tiles = lax.axis_size("vx")
    rows = courant.shape[0]
    fields = (fwd_state, adj_state, courant, decay_rate, strength)
    side, top, low = pack(*[in_hbm(field) for field in fields])
    later, side = lax.optimization_barrier((fields, side))
    side = lax.ppermute(side, "vy", [(0, 1), (1, 0)])
    corners = (HALO * FIELDS, 0)
    top = lax.dynamic_update_slice(top, side[:HALO], corners)
    low = lax.dynamic_update_slice(low, side[rows - HALO :], corners)
    below = lax.ppermute(top, "vx", [(i + 1, i) for i in range(tiles - 1)])
    above = lax.ppermute(low, "vx", [(i, i + 1) for i in range(tiles - 1)])
    slots, found_p, rim, marks, gains = run_tile(
        1.0 / groups, *later, side, in_hbm(footprint.reshape(-1)), in_hbm(owner_map.reshape(-1))
    )
    ordered, edge_p = run_rim(slots, marks, gains, rim, above, below)
    sent = lax.all_to_all(ordered, "emit", 0, 0, tiled=True)
    return finish(groups, sent, found_p, edge_p)


def solution(mesh):
    in_specs = (
        P(None, "emit", "vx", "vy"),
        P(None, "emit", "vx", "vy"),
        P("vx", "vy"),
        P("vx", "vy"),
        P("vx", "vy"),
        P("emit", "vx", "vy", None),
        P("vx", "vy", None),
    )
    out_specs = (P("emit", "vx", "vy"), P("emit", "vx", "vy"))
    return jax.shard_map(shards, mesh=mesh, in_specs=in_specs, out_specs=out_specs, check_vma=False)
```

```python
import jax
import jax.numpy as jnp
from jax import lax
from jax.experimental import pallas as pl
from jax.experimental.pallas import tpu as pltpu
from jax.sharding import PartitionSpec as P

BR = 16
BC = 128
STEPS = 4
HALO = 4
SUB = 8
LANES = 128
FIELDS = 9
TILE_AT = 2 * SUB
VMEM_LIMIT = 28 * 1024 * 1024
GROUP = (13, 37, 35, 33)


def in_hbm(array):
    return pltpu.with_memory_space_constraint(array, pltpu.HBM)


def side_kernel(fwd, adj, courant, decay, strength, side_out, cols, sem):
    rows = courant.shape[0]
    vy = lax.axis_index("vy")
    edge = pl.ds(pl.multiple_of((1 - vy) * LANES, LANES), LANES)
    copies = [(state.at[:, 0, :, edge], cols.at[pl.ds(3 * number, 3)]) for number, state in enumerate((fwd, adj))]
    copies += [(field.at[:, edge], cols.at[6 + number]) for number, field in enumerate((courant, decay, strength))]
    started = [pltpu.make_async_copy(src, dst, sem.at[n]) for n, (src, dst) in enumerate(copies)]
    for copy in started:
        copy.start()
    lane = lax.broadcasted_iota(jnp.int32, (SUB, LANES), 1)
    packed = [jnp.zeros((SUB, LANES), jnp.float32)] * (rows // SUB)
    for number, members in enumerate(((0, 1, 2), (3, 4, 5), (6,), (7,), (8,))):
        started[number].wait()
        for field in members:
            here = (lane >= HALO * field) & (lane < HALO * (field + 1))
            shift = HALO * field + HALO * (1 - vy)
            for at in range(rows // SUB):
                packed[at] = jnp.where(here, pltpu.roll(cols[field, at * SUB : (at + 1) * SUB, :], shift, 1), packed[at])
    for at in range(rows // SUB):
        side_out[at * SUB : (at + 1) * SUB, :] = packed[at]


def ends_kernel(fwd, adj, courant, decay, strength, top_out, low_out, tops, lows, sem):
    rows = courant.shape[0]
    copies = []
    for first, ends in ((0, tops), (rows - SUB, lows)):
        at = pl.ds(first, SUB)
        copies += [(state.at[:, 0, at, :], ends.at[pl.ds(3 * number, 3)]) for number, state in enumerate((fwd, adj))]
        copies += [(field.at[at, :], ends.at[6 + number]) for number, field in enumerate((courant, decay, strength))]
    started = [pltpu.make_async_copy(src, dst, sem.at[n]) for n, (src, dst) in enumerate(copies)]
    for copy in started:
        copy.start()
    for copy in started:
        copy.wait()
    for out, edges, first in ((top_out, tops, 0), (low_out, lows, SUB - HALO)):
        for field in range(FIELDS):
            out[HALO * field : HALO * (field + 1), :] = edges[field, first : first + HALO, :]
        out[HALO * FIELDS : HALO * (FIELDS + 1), :] = jnp.zeros((HALO, 2 * LANES), jnp.float32)


def pack_side(*fields):
    rows = fields[2].shape[0]
    return pl.pallas_call(
        side_kernel,
        out_shape=jax.ShapeDtypeStruct((rows, LANES), jnp.float32),
        in_specs=[pl.BlockSpec(memory_space=pltpu.HBM)] * 5,
        out_specs=pl.BlockSpec(memory_space=pltpu.VMEM),
        scratch_shapes=[pltpu.VMEM((FIELDS, rows, LANES), jnp.float32), pltpu.SemaphoreType.DMA((5,))],
        compiler_params=pltpu.CompilerParams(vmem_limit_bytes=VMEM_LIMIT),
        cost_estimate=pl.CostEstimate(flops=600000, bytes_accessed=1300000, transcendentals=0),
        name="side",
    )(*fields)


def pack_ends(*fields):
    columns = fields[2].shape[1]
    edge = jax.ShapeDtypeStruct((HALO * (FIELDS + 1), columns), jnp.float32)
    return pl.pallas_call(
        ends_kernel,
        out_shape=(edge, edge),
        in_specs=[pl.BlockSpec(memory_space=pltpu.HBM)] * 5,
        out_specs=[pl.BlockSpec(memory_space=pltpu.VMEM)] * 2,
        scratch_shapes=[
            pltpu.VMEM((FIELDS, SUB, columns), jnp.float32),
            pltpu.VMEM((FIELDS, SUB, columns), jnp.float32),
            pltpu.SemaphoreType.DMA((10,)),
        ],
        compiler_params=pltpu.CompilerParams(vmem_limit_bytes=VMEM_LIMIT),
        cost_estimate=pl.CostEstimate(flops=30000, bytes_accessed=300000, transcendentals=0),
        name="ends",
    )(*fields)


def tile_kernel(
    scale, fwd, adj, courant, decay, strength, side, footprint_in, owner_in,
    ordered, found_p, rim, marks, gains, held, coefs, starts, memories, fore, back, curves, partial, found_g,
    footprint, owner, slot_of, gain_of, list_sem,
):
    rows = courant.shape[0]
    lists = [
        pltpu.make_async_copy(footprint_in, footprint, list_sem.at[0]),
        pltpu.make_async_copy(owner_in, owner, list_sem.at[1]),
    ]
    for copy in lists:
        copy.start()
    vy = lax.axis_index("vy")
    lane = lax.broadcasted_iota(jnp.int32, (SUB, LANES), 1)
    beside = (lane >= (LANES - HALO) * vy) & (lane < (LANES - HALO) * vy + HALO)
    zero = jnp.zeros((SUB, LANES), jnp.float32)
    lane_first, lane_last = lane == 0, lane == LANES - 1
    for field in range(FIELDS):
        shift = lax.rem(LANES - HALO * field + (LANES - HALO) * vy, LANES)
        for at in range(0, rows, SUB):
            strip = pltpu.roll(side[at : at + SUB, :], shift, 1)
            held[field, 2, TILE_AT + at : TILE_AT + at + SUB, :] = jnp.where(beside, strip, zero)
        for part in range(3):
            held[field, part, SUB : 2 * SUB, :] = zero
            held[field, part, rows + 2 * SUB : rows + 3 * SUB, :] = zero
    for half in range(2):
        columns, target = slice(half * LANES, (half + 1) * LANES), slice(TILE_AT, TILE_AT + rows)
        for number in range(3):
            held[number, half, target, :] = fwd[number, 0, :, columns]
            held[3 + number, half, target, :] = adj[number, 0, :, columns]
        for number, field in enumerate((courant, decay, strength)):
            held[6 + number, half, target, :] = field[:, columns]
    for field in range(FIELDS):
        for part in range(3):
            rim[0, field, part] = held[field, part, TILE_AT : TILE_AT + 2 * SUB, :]
            rim[1, field, part] = held[field, part, rows : rows + 2 * SUB, :]

    pitch = rows // SUB + 1

    def strips(field, part, t):
        return held[field, part, pl.ds(TILE_AT - HALO + t, SUB, stride=pitch), :]

    def advance(step, base_t, group):
        final = step == STEPS
        parts = range(2) if final else range(3)
        ts = [base_t + g for g in range(group)]
        stores = []
        speed, keep, loss = {}, {}, {}
        for part in parts:
            for g, t in enumerate(ts):
                for number, of in enumerate((speed, keep, loss)):
                    if step == 1:
                        of[part, g] = strips(6 + number, part, t)
                        stores.append((coefs, (number, part, SUB + t), of[part, g]))
                    else:
                        of[part, g] = coefs[number, part, SUB + t]
        results = []
        for own, state in ((fore, 0), (back, 1)):

            def level(number, part, t, own=own, state=state):
                if number >= 2:
                    return own[number - 2, part, SUB + t]
                if step == 1:
                    return strips(3 * state + number, part, t)
                return starts[state, part, SUB + t]

            centre = {
                (part, g): level(step, part, base_t + g)
                for part in range(3)
                for g in range(-1, group + 1)
                if part in parts or 0 <= g < group
            }
            seconds, nexts = {}, {}
            for g, t in enumerate(ts):
                right = [pltpu.roll(centre[part, g], LANES - 1, 1) for part in range(3)]
                left = [pltpu.roll(centre[part, g], 1, 1) for part in range(3)]
                for part in parts:
                    west = jnp.where(lane_first, left[(part + 2) % 3], left[part])
                    east = jnp.where(lane_last, right[(part + 1) % 3], right[part])
                    now = centre[part, g]
                    curve = (centre[part, g - 1] + centre[part, g + 1]) + (east + west) - 4.0 * now
                    memory = strips(3 * state + 2, part, t) if step == 1 else memories[state, part, SUB + t]
                    memory = keep[part, g] * memory + loss[part, g] * curve
                    second = speed[part, g] * (curve - memory)
                    following = 2.0 * now - level(step - 1, part, t) + second
                    if step == 1:
                        stores.append((starts, (state, part, SUB + t), now))
                    if not final:
                        stores.append((memories, (state, part, SUB + t), memory))
                        stores.append((own, (step - 1, part, SUB + t), following))
                    seconds[part, g] = second
                    nexts[part, g] = following
            results.append((seconds, nexts))
        (seconds, nexts), (_, adjoint) = results
        for part in range(2):
            for g, t in enumerate(ts):
                if step <= 2:
                    stores.append((curves, (step - 1, part, SUB + t), seconds[part, g]))
                    continue
                other = 4 - step
                value = (
                    seconds[part, g] * back[other, part, SUB + t] + curves[other, part, SUB + t] * adjoint[part, g]
                )
                if step == 3:
                    stores.append((partial, (part, SUB + t), value))
                else:
                    rows_at = pl.ds(HALO + t, SUB, stride=pitch)
                    stores.append((found_g, (part, rows_at), partial[part, SUB + t] + value))
                    stores.append((found_p, (part, rows_at), nexts[part, g]))
        for ref, index, value in stores:
            ref[index] = value

    for step in range(1, STEPS + 1):
        margin = STEPS - step
        count = pitch + 2 * margin
        group = GROUP[step - 1]
        if count == group:
            advance(step, -margin, group)
        else:

            def turn(number, carry, step=step, margin=margin, group=group):
                advance(step, number * group - margin, group)
                return carry

            lax.fori_loop(0, count // group, turn, 0)

    for copy in lists:
        copy.wait()
    blocks = gain_of.shape[0]
    for block in range(blocks):
        gain_of[block] = jnp.float32(0.0)
    for number in range(footprint.shape[0]):
        gain_of[footprint[number]] = jnp.float32(scale)
    for number in range(blocks):
        slot_of[owner[number]] = number
        marks[number] = jnp.full((SUB, LANES), owner[number], jnp.int32)
    for number, block in enumerate((0, 1, blocks - 2, blocks - 1)):
        gains[number] = jnp.full((SUB, LANES), gain_of[block], jnp.float32)
    for block in range(blocks):
        at = SUB + block // 2 * BR
        ordered[slot_of[block]] = found_g[block % 2, at : at + BR, :] * gain_of[block]


def run_tile(scale, fwd_state, adj_state, courant, decay_rate, strength, side, footprint, owner_map):
    rows = courant.shape[0]
    strip = (3, rows // SUB + 16, SUB, LANES)
    found = (2, rows + 6 * SUB, LANES)
    blocks = owner_map.shape[0]
    return pl.pallas_call(
        lambda *refs: tile_kernel(scale, *refs),
        out_shape=(
            jax.ShapeDtypeStruct((blocks, BR, BC), jnp.float32),
            jax.ShapeDtypeStruct(found, jnp.float32),
            jax.ShapeDtypeStruct((2, FIELDS, 3, 2 * SUB, LANES), jnp.float32),
            jax.ShapeDtypeStruct((blocks, SUB, LANES), jnp.int32),
            jax.ShapeDtypeStruct((4, SUB, LANES), jnp.float32),
        ),
        in_specs=[pl.BlockSpec(memory_space=pltpu.VMEM)] * 6 + [pl.BlockSpec(memory_space=pltpu.HBM)] * 2,
        out_specs=[pl.BlockSpec(memory_space=pltpu.VMEM)] * 5,
        scratch_shapes=[
            pltpu.VMEM((FIELDS, 3, rows + 7 * SUB, LANES), jnp.float32),
            pltpu.VMEM((3,) + strip, jnp.float32),
            pltpu.VMEM((2,) + strip, jnp.float32),
            pltpu.VMEM((2,) + strip, jnp.float32),
            pltpu.VMEM((STEPS - 1,) + strip, jnp.float32),
            pltpu.VMEM((STEPS - 1,) + strip, jnp.float32),
            pltpu.VMEM((2,) + strip, jnp.float32),
            pltpu.VMEM(strip, jnp.float32),
            pltpu.VMEM(found, jnp.float32),
            pltpu.SMEM(footprint.shape, jnp.int32),
            pltpu.SMEM((blocks,), jnp.int32),
            pltpu.SMEM((blocks,), jnp.int32),
            pltpu.SMEM((blocks,), jnp.float32),
            pltpu.SemaphoreType.DMA((2,)),
        ],
        compiler_params=pltpu.CompilerParams(vmem_limit_bytes=VMEM_LIMIT),
        cost_estimate=pl.CostEstimate(flops=14000000, bytes_accessed=3500000, transcendentals=0),
        name="tile",
    )(fwd_state, adj_state, courant, decay_rate, strength, side, footprint, owner_map)


def rim_kernel(slots, marks, gains, rim, above, below, ordered, edge_p):
    vy = lax.axis_index("vy")
    lane = lax.broadcasted_iota(jnp.int32, (SUB, LANES), 1)
    sub = lax.broadcasted_iota(jnp.int32, (SUB, LANES), 0)
    beside = (lane >= (LANES - HALO) * vy) & (lane < (LANES - HALO) * vy + HALO)
    zero = jnp.zeros((SUB, LANES), jnp.float32)
    lane_first, lane_last = lane == 0, lane == LANES - 1
    first, last = sub == 0, sub == SUB - 1

    def halo_of(field, part, low):
        source = below if low else above
        last_pair = HALO * (FIELDS - 1)
        at = last_pair if part == 2 else (field // 2) * SUB
        value = source[at : at + SUB, (part % 2) * LANES : (part % 2 + 1) * LANES]
        in_lower_rows = part == 2 or field % 2 == 1
        if in_lower_rows == low:
            value = pltpu.roll(value, HALO, 0)
        value = jnp.where((sub < HALO) if low else (sub >= HALO), value, zero)
        if part == 2:
            shift = lax.rem(LANES - HALO * field + (LANES - HALO) * vy, LANES)
            value = jnp.where(beside, pltpu.roll(value, shift, 1), zero)
        return value

    def window(field, low):
        result = []
        for chunk in range(3):
            if low:
                row = [halo_of(field, p, True) if chunk == 2 else rim[1, field, p, chunk * SUB : (chunk + 1) * SUB, :] for p in range(3)]
            else:
                row = [halo_of(field, p, False) if chunk == 0 else rim[0, field, p, (chunk - 1) * SUB : chunk * SUB, :] for p in range(3)]
            result.append(row)
        return result

    edges = {}
    for low in (False, True):
        speed, keep, loss = (window(field, low) for field in (6, 7, 8))
        states = [[window(3 * state + field, low) for field in range(3)] for state in range(2)]
        levels = ([], [])
        curves = []
        for step in range(1, STEPS + 1):
            chunks = (1,) if step == STEPS else (0, 1, 2)
            for state in range(2):
                old, new, memory = states[state]
                up = [[pltpu.roll(value, 1, 0) for value in row] for row in new]
                down = [[pltpu.roll(value, SUB - 1, 0) for value in row] for row in new]
                memories = [list(row) for row in memory]
                nexts = [list(row) for row in new]
                for chunk in chunks:
                    right = [pltpu.roll(value, LANES - 1, 1) for value in new[chunk]]
                    left = [pltpu.roll(value, 1, 1) for value in new[chunk]]
                    for part in range(2) if step == STEPS else range(3):
                        now = new[chunk][part]
                        north = jnp.where(first, up[chunk - 1][part] if chunk > 0 else zero, up[chunk][part])
                        south = jnp.where(last, down[chunk + 1][part] if chunk < 2 else zero, down[chunk][part])
                        west = jnp.where(lane_first, left[(part + 2) % 3], left[part])
                        east = jnp.where(lane_last, right[(part + 1) % 3], right[part])
                        curve = (north + south) + (east + west) - 4.0 * now
                        held = keep[chunk][part] * memory[chunk][part] + loss[chunk][part] * curve
                        second = speed[chunk][part] * (curve - held)
                        memories[chunk][part] = held
                        nexts[chunk][part] = 2.0 * now - old[chunk][part] + second
                        if state == 0 and chunk == 1 and part < 2:
                            curves.append(second)
                levels[state].append(nexts[1])
                states[state] = [new, nexts, memories]
        at = slice(SUB, 2 * SUB) if low else slice(0, SUB)
        for part in range(2):
            adjoint = [level[part] for level in levels[1]]
            seconds = curves[part::2]
            value = seconds[2] * adjoint[1] + seconds[1] * adjoint[2]
            value = value + (seconds[3] * adjoint[0] + seconds[0] * adjoint[3])
            edge_p[at, part * LANES : (part + 1) * LANES] = levels[0][STEPS - 1][part]
            edges[low, part] = value * gains[2 * low + part]

    blocks = slots.shape[0]
    for slot in range(blocks):
        block = marks[slot]
        high, low = slots[slot, 0:SUB, :], slots[slot, SUB:BR, :]
        for part in range(2):
            high = jnp.where(block == part, edges[False, part], high)
            low = jnp.where(block == blocks - 2 + part, edges[True, part], low)
        ordered[slot, 0:SUB, :] = high
        ordered[slot, SUB:BR, :] = low


def run_rim(slots, marks, gains, rim, above, below):
    return pl.pallas_call(
        rim_kernel,
        out_shape=(
            jax.ShapeDtypeStruct(slots.shape, jnp.float32),
            jax.ShapeDtypeStruct((2 * SUB, above.shape[1]), jnp.float32),
        ),
        in_specs=[pl.BlockSpec(memory_space=pltpu.VMEM)] * 6,
        out_specs=[pl.BlockSpec(memory_space=pltpu.VMEM)] * 2,
        compiler_params=pltpu.CompilerParams(vmem_limit_bytes=VMEM_LIMIT),
        cost_estimate=pl.CostEstimate(flops=2000000, bytes_accessed=1000000, transcendentals=0),
        name="rim",
    )(slots, marks, gains, rim, above, below)


def finish_kernel(sent, found_p, edge_p, gradient, pressure, total, sem):
    rows = pressure.shape[1]
    inner = rows - 2 * SUB
    copies = [
        (edge_p.at[pl.ds(0, SUB), :], pressure.at[0, pl.ds(0, SUB), :]),
        (edge_p.at[pl.ds(SUB, SUB), :], pressure.at[0, pl.ds(rows - SUB, SUB), :]),
    ]
    for half in range(2):
        columns = pl.ds(half * LANES, LANES)
        copies.append((found_p.at[half, pl.ds(2 * SUB, inner), :], pressure.at[0, pl.ds(SUB, inner), columns]))
    copies = [pltpu.make_async_copy(src, dst, sem.at[n]) for n, (src, dst) in enumerate(copies)]
    for copy in copies:
        copy.start()
    held = gradient.shape[0]
    for slot in range(held):
        terms = [sent[number] for number in range(slot, sent.shape[0], held)]
        while len(terms) > 1:
            joined = [one + two for one, two in zip(terms[::2], terms[1::2])]
            terms = joined + terms[2 * len(joined) :]
        total[slot] = terms[0]
    last = pltpu.make_async_copy(total, gradient, sem.at[4])
    last.start()
    last.wait()
    for copy in copies:
        copy.wait()


def finish(groups, sent, found_p, edge_p):
    gradient = (sent.shape[0] // groups, BR, BC)
    rows, columns = found_p.shape[1] - 6 * SUB, edge_p.shape[1]
    return pl.pallas_call(
        finish_kernel,
        out_shape=(
            jax.ShapeDtypeStruct(gradient, jnp.float32),
            jax.ShapeDtypeStruct((1, rows, columns), jnp.float32),
        ),
        in_specs=[pl.BlockSpec(memory_space=pltpu.VMEM)] * 3,
        out_specs=[pl.BlockSpec(memory_space=pltpu.HBM)] * 2,
        scratch_shapes=[pltpu.VMEM(gradient, jnp.float32), pltpu.SemaphoreType.DMA((5,))],
        compiler_params=pltpu.CompilerParams(vmem_limit_bytes=VMEM_LIMIT),
        cost_estimate=pl.CostEstimate(flops=70000, bytes_accessed=800000, transcendentals=0),
        name="finish",
    )(sent, found_p, edge_p)


def shards(fwd_state, adj_state, courant, decay_rate, strength, footprint, owner_map):
    groups = lax.axis_size("emit")
    tiles = lax.axis_size("vx")
    rows = courant.shape[0]
    fields = (fwd_state, adj_state, courant, decay_rate, strength)
    held = [in_hbm(field) for field in fields]
    strips = pack_side(*held)
    later, strips = lax.optimization_barrier((fields, strips))
    side = lax.ppermute(strips, "vy", [(0, 1), (1, 0)])
    top, low = pack_ends(*[in_hbm(field) for field in later])
    corners = (HALO * FIELDS, 0)
    top = lax.dynamic_update_slice(top, side[:HALO], corners)
    low = lax.dynamic_update_slice(low, side[rows - HALO :], corners)
    below = lax.ppermute(top, "vx", [(i + 1, i) for i in range(tiles - 1)])
    above = lax.ppermute(low, "vx", [(i, i + 1) for i in range(tiles - 1)])
    slots, found_p, rim, marks, gains = run_tile(
        1.0 / groups, *later, side, in_hbm(footprint.reshape(-1)), in_hbm(owner_map.reshape(-1))
    )
    ordered, edge_p = run_rim(slots, marks, gains, rim, above, below)
    sent = lax.all_to_all(ordered, "emit", 0, 0, tiled=True)
    return finish(groups, sent, found_p, edge_p)


def solution(mesh):
    in_specs = (
        P(None, "emit", "vx", "vy"),
        P(None, "emit", "vx", "vy"),
        P("vx", "vy"),
        P("vx", "vy"),
        P("vx", "vy"),
        P("emit", "vx", "vy", None),
        P("vx", "vy", None),
    )
    out_specs = (P("emit", "vx", "vy"), P("emit", "vx", "vy"))
    return jax.shard_map(shards, mesh=mesh, in_specs=in_specs, out_specs=out_specs, check_vma=False)
```
